512 devices in a mesh: dp: 128 (over y, z, core), mp: 4 (over x).
Axes of the slice: x: 4, y: 8, z: 8, core: 2. Of those that a mesh axis runs over, the one named last changes fastest.
Arguments:
- query_hidden: bfloat16 [4096, 32, 768], P('dp', None, 'mp'), may hold values from -6 to 6
- query_proj: bfloat16 [768, 128], P('mp'), may hold values from -0.21875 to 0.21875
- passages: bfloat16 [8192, 128, 128], P(('dp', 'mp')), may hold values from -6 to 6
- teacher: float32 [4096, 4, 64], P('dp'), may hold values from -8 to 8
- neg_blocks: int32 [4096, 4], P('dp'), may hold values from 0 to 127, all different within a row; in each aligned block of 32 rows (0 to 31, 32 to 63, ...) at most 2 rows name the same one
Outputs:
- kl_loss: float32 [4096], P('dp')
The draws below stay inside these ranges and needn't reach their ends.
Inputs may be any that keep to these rules, and one draw needn't show every extreme that they name: `neg_blocks`: each query names 4 different blocks. Among the 32 queries of one dp index no block is named more than 2 times, and some block is named exactly 2 times.
All inputs are finite; a program needn't handle non-finite values.
Results may differ from the reference program's by a relative error of at most 0.0003.
Values may be sent and summed in bfloat16 or wider, within the bound.
No kernel may reach another device: no remote copies, remote signals or barrier semaphores. Data moves between devices by JAX's collectives and lax.ppermute only.
A program may use at most 64 MiB of HBM per device.

```python
import math
import jax
import jax.numpy as jnp
import numpy as np
from jax import lax

H = 768
E = 128
QT = 32
PT = 128
BP = 64
NB = 4
QD = 32
QUERIES = 4096
BLOCKS = 128
PASSAGES = 8192
CAP = 2


def level_of(own_key, extent, pieces, least, top_value):
    def one(dim, shards_of):
        draws = jax.random.uniform(jax.random.fold_in(jax.random.fold_in(own_key, 6), dim), (shards_of,), jnp.float32, least / len(pieces), top_value / len(pieces))
        return jnp.repeat(jnp.exp(draws), extent[dim] // shards_of).reshape((-1,) + (1,) * (len(extent) - dim - 1))

    factor_of = one(*pieces[0])
    for cut in pieces[1:]:
        factor_of = factor_of * one(*cut)
    return factor_of


def deal_out(stream_key, own, number, rows, amount, top, reach, lean):
    order = jax.random.permutation(stream_key, amount)
    heavy_load, ordinary = load_shares(amount, rows * top, reach, lean, True), load_shares(amount, rows * top, reach, lean, False)
    places = jnp.arange(amount)

    def named(lengths, offset_by):
        used = int((lengths > 0).sum())
        fixed = max(1, used // 4)
        passed = fixed + (places - fixed + offset_by * (used - fixed)) % max(1, amount - fixed)
        return jnp.zeros((amount,), jnp.int32).at[order[jnp.where(places < fixed, places, passed)]].set(jnp.asarray(lengths, jnp.int32))

    lengths = jnp.where(number % 4 == 0, named(heavy_load, number // 4), named(ordinary, number - number // 4 - 1))
    mixed = jax.random.permutation(jax.random.fold_in(own, 3), amount)
    donor, receiver = mixed[0:amount // 2 * 2:2], mixed[1:amount // 2 * 2:2]
    room = jnp.minimum(lengths[donor] - 1, reach - lengths[receiver]) // 2
    room = jnp.where((donor == order[0]) | (receiver == order[0]) | (lengths[receiver] == 0), 0, jnp.maximum(room, 0))
    passed = jax.random.randint(jax.random.fold_in(own, 4), (amount // 2,), 0, 1 << 20) % (room + 1)
    lengths = lengths.at[donor].add(-passed).at[receiver].add(passed)
    members = jnp.searchsorted(jnp.cumsum(lengths), jnp.arange(rows * top), side="right").astype(jnp.int32)
    grid = members.reshape(top, rows).T
    grid = grid[jax.random.permutation(jax.random.fold_in(own, 1), rows)]
    offset_by = jax.random.randint(jax.random.fold_in(own, 2), (rows, 1), 0, top)
    return jnp.take_along_axis(grid, (jnp.arange(top)[None, :] + offset_by) % top, axis=1)


def load_shares(number_of, total, most, slope, full):
    weights = [(1 << 20) // math.isqrt(rank ** slope) + 1 for rank in range(1, number_of + 1)]
    largest = most if full else min(most, max(-(-total // number_of), total * weights[0] // sum(weights)))
    least = 1 if total - largest >= number_of - 1 else 0
    given, surplus = [largest] + [least] * (number_of - 1), total - largest - least * (number_of - 1)
    while surplus > 0:
        candidates = [i for i in range(1, number_of) if given[i] < largest] or [i for i in range(1, number_of) if given[i] < most]
        mass, remaining = sum([weights[i] for i in candidates]), surplus
        for i in candidates:
            more = min(most - given[i], max(1, remaining * weights[i] // mass), surplus)
            given[i] = given[i] + more
            surplus = surplus - more
    return np.array(given)


def gaussian(stream_key, dims, deviation, bound, pieces=(), dtype=jnp.bfloat16):
    result = jax.random.normal(stream_key, dims, jnp.float32) * deviation
    if len(pieces) > 0:
        result = level_of(stream_key, dims, pieces, -0.22, 0.18) * result
    return jnp.clip(result, min=-bound, max=bound).astype(dtype)


def setup_inputs(seed: int = 0) -> dict:
    keys = jax.random.split(jax.random.key(seed), 6)
    query_hidden = gaussian(keys[0], (QUERIES, QT, H), 1.0, 6.0, ((0, 128), (2, 4)))
    query_proj = gaussian(keys[1], (H, E), H ** -0.5, 0.21875, ((0, 4),))
    passages = gaussian(keys[2], (PASSAGES, PT, E), 1.0, 6.0, ((0, 512),))
    teacher = gaussian(keys[3], (QUERIES, NB, BP), 2.0, 8.0, ((0, 128),), jnp.float32)
    neg_blocks_keys = jax.random.split(jax.random.fold_in(keys[4], 1), QUERIES // QD)
    neg_blocks_turns = jax.random.permutation(jax.random.fold_in(keys[4], 3), QUERIES // QD)
    neg_blocks = jax.vmap(lambda own, number: deal_out(jax.random.fold_in(keys[4], 2), own, number, QD, BLOCKS, NB, CAP, 2))(neg_blocks_keys, neg_blocks_turns).reshape((QUERIES, NB))
    return {"query_hidden": query_hidden, "query_proj": query_proj, "passages": passages, "teacher": teacher, "neg_blocks": neg_blocks}


softness = 0.1

def unit_rows(values):
    return values * lax.rsqrt(lax.optimization_barrier(jnp.sum(values * values, axis=-1, keepdims=True)) + 1e-06)

def reference(query_hidden, query_proj, passages, teacher, neg_blocks):
    projected = jnp.einsum('qth,he->qte', query_hidden.astype(jnp.float32), query_proj.astype(jnp.float32))
    query_vecs = unit_rows(projected).astype(jnp.bfloat16)
    passage_vecs = unit_rows(passages.astype(jnp.float32)).astype(jnp.bfloat16)
    blocks = passage_vecs.reshape(BLOCKS, BP, PT, E)

    def query_scores(query_pair):
        vectors, chosen_ids = query_pair
        chosen = blocks[chosen_ids]
        sims = jnp.einsum('ie,kpje->ikpj', vectors.astype(jnp.float32), chosen.astype(jnp.float32))
        softened = softness * jnp.log(lax.optimization_barrier(jnp.sum(jnp.exp(sims / softness), axis=-1)))
        return lax.optimization_barrier(jnp.sum(softened, axis=0))
    student = lax.map(query_scores, (query_vecs, neg_blocks))
    teacher_logp = teacher - jnp.log(lax.optimization_barrier(jnp.sum(jnp.exp(teacher), axis=(1, 2), keepdims=True)))
    kl_loss = lax.optimization_barrier(jnp.sum(jnp.exp(teacher_logp) * (teacher_logp - student), axis=(1, 2))) + jnp.log(lax.optimization_barrier(jnp.sum(jnp.exp(student), axis=(1, 2))))
    return kl_loss
```

```python
import functools
import math

import jax
import jax.numpy as jnp
from jax import lax
from jax.experimental import pallas as pl
from jax.experimental.pallas import tpu as pltpu
from jax.sharding import PartitionSpec as P


SOFTNESS = 0.1
EXP2_SCALE = math.log2(math.e) / SOFTNESS
EPS = 1e-6
VMEM = pl.BlockSpec(memory_space=pltpu.VMEM)
SMEM = pl.BlockSpec(memory_space=pltpu.SMEM)


def unit_rows(values):
    return values * lax.rsqrt(jnp.sum(values * values, axis=-1, keepdims=True) + EPS)


def project_kernel(parts, hidden_ref, proj_ref, out_ref):
    _, queries, share, embed = out_ref.shape
    projected = jnp.dot(hidden_ref[...], proj_ref[...], preferred_element_type=jnp.float32)
    projected = projected.reshape(queries, parts, share, embed)
    for part in range(parts):
        out_ref[part] = projected[:, part]


def passage_kernel(passages_ref, out_ref):
    out_ref[...] = unit_rows(passages_ref[...].astype(jnp.float32)).astype(jnp.bfloat16)


def pack_kernel(source_ref, partial_ref, out_ref, vecs):
    share = partial_ref.shape[2]
    total = partial_ref[0]
    for part in range(1, partial_ref.shape[0]):
        total = total + partial_ref[part]
    vecs[...] = unit_rows(total)
    capacity = out_ref.shape[1] // share

    def place(owner, carry):
        rows = [vecs[source_ref[owner * capacity + rank]] for rank in range(capacity)]
        out_ref[owner] = jnp.concatenate(rows, axis=0).astype(jnp.bfloat16)
        return carry

    lax.fori_loop(0, out_ref.shape[0], place, 0, unroll=8)


def turn_kernel(capacity, slots_ref, out_ref, wide):
    share, width, _ = out_ref.shape
    dp = width // capacity
    wide[...] = slots_ref[...].astype(jnp.float32)
    for token in range(share):
        for rank in range(capacity):
            rows = wide[pl.ds(rank * share + token, dp, stride=capacity * share), :]
            out_ref[token, rank * dp : (rank + 1) * dp] = rows.astype(jnp.bfloat16)


def score_kernel(capacity, *refs):
    slots_ref, *passage_refs, out_ref, sums = refs
    parts = len(passage_refs)
    share, count, _, width = sums.shape
    own = count // parts
    tokens = passage_refs[0].shape[0] // own
    dp = width // capacity
    group = 8
    mine = lax.axis_index("mp")

    def one_token(token, carry):
        vecs = slots_ref[token]
        for part in range(parts):
            for first in range(0, own, group):
                sims = lax.dot_general(
                    passage_refs[part][first * tokens : (first + group) * tokens, :],
                    vecs,
                    (((1,), (1,)), ((), ())),
                    preferred_element_type=jnp.float32,
                )
                raised = jnp.exp2(sims * EXP2_SCALE)
                place = lax.rem(mine + (parts - part), parts) * own + first
                sums[token, pl.ds(place, group)] = jnp.sum(
                    raised.reshape(group, tokens // 8, 8, width), axis=1
                )
        return carry

    lax.fori_loop(0, share, one_token, 0, unroll=2)
    logs = jnp.log(jnp.sum(sums[0], axis=1))
    for token in range(1, share):
        logs = logs + jnp.log(jnp.sum(sums[token], axis=1))
    logs = logs * SOFTNESS
    stacked = jnp.concatenate(
        [logs[:, rank * dp : (rank + 1) * dp] for rank in range(capacity)], axis=0
    )
    out_ref[...] = stacked.T


def home_kernel(owner_ref, rank_ref, scores_ref, out_ref):
    parts, pairs, queries, width = out_ref.shape
    count = width // 2
    lane = lax.broadcasted_iota(jnp.int32, (1, width), 1)

    def one_query(query, carry):
        for pair in range(pairs):
            halves = []
            for half in range(2):
                row = (query * pairs + pair) * 2 + half
                values = scores_ref[pl.ds(owner_ref[row], 1), :]
                turned = pltpu.roll(values, count, 1)
                halves.append(jnp.where(rank_ref[row] == half, values, turned))
            joined = jnp.where(lane < count, halves[0], halves[1])
            for part in range(parts):
                out_ref[part, pair, pl.ds(query, 1), :] = joined
        return carry

    lax.fori_loop(0, queries, one_query, 0, unroll=4)


def loss_kernel(partial_ref, teacher_ref, out_ref):
    pairs = partial_ref.shape[1]
    summed = partial_ref[0]
    for part in range(1, partial_ref.shape[0]):
        summed = summed + partial_ref[part]
    student = jnp.concatenate([summed[pair] for pair in range(pairs)], axis=1)
    teacher = teacher_ref[...]
    teacher_logp = teacher - jnp.log(jnp.sum(jnp.exp(teacher), axis=1, keepdims=True))
    loss = jnp.sum(jnp.exp(teacher_logp) * (teacher_logp - student), axis=1, keepdims=True)
    loss = loss + jnp.log(jnp.sum(jnp.exp(student), axis=1, keepdims=True))
    queries = loss.shape[0]
    out_ref[...] = jnp.broadcast_to(loss, (queries, 128)).T[:1]


def scored_loss(query_hidden, query_proj, passages, teacher, neg_blocks):
    dp = lax.axis_size("dp")
    mp = lax.axis_size("mp")
    queries, tokens, features = query_hidden.shape
    embed = query_proj.shape[1]
    picks = neg_blocks.shape[1]
    rows = queries * picks
    capacity = 2
    share = tokens // mp
    own_count, passage_tokens, _ = passages.shape
    count = own_count * mp

    partial = pl.pallas_call(
        functools.partial(project_kernel, mp),
        out_shape=jax.ShapeDtypeStruct((mp, queries, share, embed), jnp.float32),
        in_specs=[VMEM, VMEM],
        out_specs=VMEM,
        name="project",
    )(query_hidden.reshape(queries * tokens, features), query_proj)
    partial = lax.all_to_all(
        partial.reshape(mp, queries * share, embed), "mp", 0, 0, tiled=True
    ).reshape(mp, queries, share, embed)

    own_vecs = pl.pallas_call(
        passage_kernel,
        out_shape=jax.ShapeDtypeStruct((own_count * passage_tokens, embed), jnp.bfloat16),
        in_specs=[VMEM],
        out_specs=VMEM,
        name="passages",
    )(passages.reshape(own_count * passage_tokens, embed))
    passage_vecs = [own_vecs]
    for shift in range(1, mp):
        ring = [(place, (place + shift) % mp) for place in range(mp)]
        passage_vecs.append(lax.ppermute(own_vecs, "mp", ring))

    owners = neg_blocks.reshape(rows)
    row_ids = jnp.arange(rows, dtype=jnp.int32)
    earlier = (owners[:, None] == owners[None, :]) & (row_ids[None, :] < row_ids[:, None])
    ranks = jnp.sum(earlier.astype(jnp.int32), axis=1)
    slot_ids = owners * capacity + ranks
    slots = jnp.arange(dp * capacity, dtype=jnp.int32)
    source = jnp.sum(
        jnp.where(slots[:, None] == slot_ids[None, :], (row_ids // picks)[None, :], 0), axis=1
    )

    outgoing = pl.pallas_call(
        pack_kernel,
        out_shape=jax.ShapeDtypeStruct((dp, capacity * share, embed), jnp.bfloat16),
        in_specs=[SMEM, VMEM],
        out_specs=VMEM,
        scratch_shapes=[pltpu.VMEM((queries, share, embed), jnp.float32)],
        name="pack",
    )(source, partial)
    arrived = lax.all_to_all(outgoing, "dp", 0, 0, tiled=True)

    turned = pl.pallas_call(
        functools.partial(turn_kernel, capacity),
        out_shape=jax.ShapeDtypeStruct((share, capacity * dp, embed), jnp.bfloat16),
        in_specs=[VMEM],
        out_specs=VMEM,
        scratch_shapes=[pltpu.VMEM((dp * capacity * share, embed), jnp.float32)],
        name="turn",
    )(arrived.reshape(dp * capacity * share, embed))
    scores = pl.pallas_call(
        functools.partial(score_kernel, capacity),
        out_shape=jax.ShapeDtypeStruct((dp, capacity * count), jnp.float32),
        in_specs=[VMEM] * (1 + mp),
        out_specs=VMEM,
        scratch_shapes=[pltpu.VMEM((share, count, 8, dp * capacity), jnp.float32)],
        name="score",
    )(turned, *passage_vecs)
    returned = lax.all_to_all(
        scores.reshape(dp, 1, capacity * count), "dp", 0, 0, tiled=True
    ).reshape(dp, capacity * count)

    home = pl.pallas_call(
        home_kernel,
        out_shape=jax.ShapeDtypeStruct((mp, picks // 2, queries, 2 * count), jnp.float32),
        in_specs=[SMEM, SMEM, VMEM],
        out_specs=VMEM,
        name="home",
    )(owners, ranks, returned)
    home = lax.all_to_all(home, "mp", 0, 0, tiled=True)

    loss = pl.pallas_call(
        loss_kernel,
        out_shape=jax.ShapeDtypeStruct((1, queries), jnp.float32),
        in_specs=[VMEM, VMEM],
        out_specs=VMEM,
        name="loss",
    )(home, teacher.reshape(queries, picks * count))
    return loss.reshape(queries)


def solution(mesh):
    in_specs = (
        P("dp", None, "mp"),
        P("mp", None),
        P(("dp", "mp"), None, None),
        P("dp", None, None),
        P("dp", None),
    )
    return jax.shard_map(
        scored_loss, mesh=mesh, in_specs=in_specs, out_specs=P("dp"), check_vma=False
    )
```

```python
import functools
import math

import jax
import jax.numpy as jnp
from jax import lax
from jax.experimental import pallas as pl
from jax.experimental.pallas import tpu as pltpu
from jax.sharding import PartitionSpec as P


SOFTNESS = 0.1
EXP2_SCALE = math.log2(math.e) / SOFTNESS
EPS = 1e-6
VMEM = pl.BlockSpec(memory_space=pltpu.VMEM)
SMEM = pl.BlockSpec(memory_space=pltpu.SMEM)


def unit_rows(values):
    return values * lax.rsqrt(jnp.sum(values * values, axis=-1, keepdims=True) + EPS)


def project_kernel(parts, hidden_ref, proj_ref, out_ref):
    _, queries, share, embed = out_ref.shape
    projected = jnp.dot(hidden_ref[...], proj_ref[...], preferred_element_type=jnp.float32)
    projected = projected.reshape(queries, parts, share, embed)
    for part in range(parts):
        out_ref[part] = projected[:, part]


def passage_kernel(passages_ref, out_ref):
    out_ref[...] = unit_rows(passages_ref[...].astype(jnp.float32)).astype(jnp.bfloat16)


def pack_kernel(source_ref, partial_ref, out_ref, vecs):
    share = partial_ref.shape[2]
    total = partial_ref[0]
    for part in range(1, partial_ref.shape[0]):
        total = total + partial_ref[part]
    vecs[...] = unit_rows(total)
    capacity = out_ref.shape[1] // share

    def place(owner, carry):
        rows = [vecs[source_ref[owner * capacity + rank]] for rank in range(capacity)]
        out_ref[owner] = jnp.concatenate(rows, axis=0).astype(jnp.bfloat16)
        return carry

    lax.fori_loop(0, out_ref.shape[0], place, 0, unroll=8)


def score_kernel(capacity, *refs):
    slots_ref, *passage_refs, out_ref, wide, turned, sums = refs
    parts = len(passage_refs)
    share, count, _, width = sums.shape
    own = count // parts
    tokens = passage_refs[0].shape[0] // own
    dp = width // capacity
    group = 8
    mine = lax.axis_index("mp")
    wide[...] = slots_ref[...].astype(jnp.float32)
    for token in range(share):
        for rank in range(capacity):
            rows = wide[pl.ds(rank * share + token, dp, stride=capacity * share), :]
            turned[token, rank * dp : (rank + 1) * dp] = rows.astype(jnp.bfloat16)

    def one_token(token, carry):
        vecs = turned[token]
        for part in range(parts):
            for first in range(0, own, group):
                sims = lax.dot_general(
                    passage_refs[part][first * tokens : (first + group) * tokens, :],
                    vecs,
                    (((1,), (1,)), ((), ())),
                    preferred_element_type=jnp.float32,
                )
                raised = jnp.exp2(sims * EXP2_SCALE)
                place = lax.rem(mine + (parts - part), parts) * own + first
                sums[token, pl.ds(place, group)] = jnp.sum(
                    raised.reshape(group, tokens // 8, 8, width), axis=1
                )
        return carry

    lax.fori_loop(0, share, one_token, 0, unroll=2)
    logs = jnp.log(jnp.sum(sums[0], axis=1))
    for token in range(1, share):
        logs = logs + jnp.log(jnp.sum(sums[token], axis=1))
    logs = logs * SOFTNESS
    stacked = jnp.concatenate(
        [logs[:, rank * dp : (rank + 1) * dp] for rank in range(capacity)], axis=0
    )
    scores = stacked.T
    for part in range(parts):
        out_ref[pl.ds(part, dp, stride=parts), :] = scores


def loss_kernel(owner_ref, rank_ref, partial_ref, teacher_ref, out_ref, scores, student):
    pairs, queries, width = student.shape
    count = width // 2
    dp = scores.shape[0]
    parts = partial_ref.shape[0] // dp
    total = partial_ref[pl.ds(0, dp, stride=parts), :]
    for part in range(1, parts):
        total = total + partial_ref[pl.ds(part, dp, stride=parts), :]
    scores[...] = total
    lane = lax.broadcasted_iota(jnp.int32, (1, width), 1)

    def one_query(query, carry):
        for pair in range(pairs):
            halves = []
            for half in range(2):
                row = (query * pairs + pair) * 2 + half
                values = scores[pl.ds(owner_ref[row], 1), :]
                turned = pltpu.roll(values, count, 1)
                halves.append(jnp.where(rank_ref[row] == half, values, turned))
            student[pair, pl.ds(query, 1), :] = jnp.where(lane < count, halves[0], halves[1])
        return carry

    lax.fori_loop(0, queries, one_query, 0, unroll=8)
    chosen = jnp.concatenate([student[pair] for pair in range(pairs)], axis=1)
    teacher = teacher_ref[...]
    teacher_logp = teacher - jnp.log(jnp.sum(jnp.exp(teacher), axis=1, keepdims=True))
    loss = jnp.sum(jnp.exp(teacher_logp) * (teacher_logp - chosen), axis=1, keepdims=True)
    loss = loss + jnp.log(jnp.sum(jnp.exp(chosen), axis=1, keepdims=True))
    out_ref[...] = jnp.broadcast_to(loss, (queries, 128)).T[:1]


def scored_loss(query_hidden, query_proj, passages, teacher, neg_blocks):
    dp = lax.axis_size("dp")
    mp = lax.axis_size("mp")
    queries, tokens, features = query_hidden.shape
    embed = query_proj.shape[1]
    picks = neg_blocks.shape[1]
    rows = queries * picks
    capacity = 2
    share = tokens // mp
    own_count, passage_tokens, _ = passages.shape
    count = own_count * mp

    partial = pl.pallas_call(
        functools.partial(project_kernel, mp),
        out_shape=jax.ShapeDtypeStruct((mp, queries, share, embed), jnp.float32),
        in_specs=[VMEM, VMEM],
        out_specs=VMEM,
        name="project",
    )(query_hidden.reshape(queries * tokens, features), query_proj)
    partial = lax.all_to_all(
        partial.reshape(mp, queries * share, embed), "mp", 0, 0, tiled=True
    ).reshape(mp, queries, share, embed)

    own_vecs = pl.pallas_call(
        passage_kernel,
        out_shape=jax.ShapeDtypeStruct((own_count * passage_tokens, embed), jnp.bfloat16),
        in_specs=[VMEM],
        out_specs=VMEM,
        name="passages",
    )(passages.reshape(own_count * passage_tokens, embed))
    passage_vecs = [own_vecs]
    for shift in range(1, mp):
        ring = [(place, (place + shift) % mp) for place in range(mp)]
        passage_vecs.append(lax.ppermute(own_vecs, "mp", ring))

    owners = neg_blocks.reshape(rows)
    row_ids = jnp.arange(rows, dtype=jnp.int32)
    earlier = (owners[:, None] == owners[None, :]) & (row_ids[None, :] < row_ids[:, None])
    ranks = jnp.sum(earlier.astype(jnp.int32), axis=1)
    slot_ids = owners * capacity + ranks
    slots = jnp.arange(dp * capacity, dtype=jnp.int32)
    source = jnp.sum(
        jnp.where(slots[:, None] == slot_ids[None, :], (row_ids // picks)[None, :], 0), axis=1
    )

    outgoing = pl.pallas_call(
        pack_kernel,
        out_shape=jax.ShapeDtypeStruct((dp, capacity * share, embed), jnp.bfloat16),
        in_specs=[SMEM, VMEM],
        out_specs=VMEM,
        scratch_shapes=[pltpu.VMEM((queries, share, embed), jnp.float32)],
        name="pack",
    )(source, partial)
    arrived = lax.all_to_all(outgoing, "dp", 0, 0, tiled=True)

    scores = pl.pallas_call(
        functools.partial(score_kernel, capacity),
        out_shape=jax.ShapeDtypeStruct((dp * mp, capacity * count), jnp.float32),
        in_specs=[VMEM] * (1 + mp),
        out_specs=VMEM,
        scratch_shapes=[
            pltpu.VMEM((dp * capacity * share, embed), jnp.float32),
            pltpu.VMEM((share, dp * capacity, embed), jnp.bfloat16),
            pltpu.VMEM((share, count, 8, dp * capacity), jnp.float32),
        ],
        name="score",
    )(arrived.reshape(dp * capacity * share, embed), *passage_vecs)
    returned = lax.all_to_all(
        scores.reshape(dp * mp, 1, capacity * count), ("dp", "mp"), 0, 0, tiled=True
    ).reshape(dp * mp, capacity * count)

    loss = pl.pallas_call(
        loss_kernel,
        out_shape=jax.ShapeDtypeStruct((1, queries), jnp.float32),
        in_specs=[SMEM, SMEM, VMEM, VMEM],
        out_specs=VMEM,
        scratch_shapes=[
            pltpu.VMEM((dp, capacity * count), jnp.float32),
            pltpu.VMEM((picks // 2, queries, 2 * count), jnp.float32),
        ],
        name="loss",
    )(owners, ranks, returned, teacher.reshape(queries, picks * count))
    return loss.reshape(queries)


def solution(mesh):
    in_specs = (
        P("dp", None, "mp"),
        P("mp", None),
        P(("dp", "mp"), None, None),
        P("dp", None, None),
        P("dp", None),
    )
    return jax.shard_map(
        scored_loss, mesh=mesh, in_specs=in_specs, out_specs=P("dp"), check_vma=False
    )
```

```python
import functools
import math

import jax
import jax.numpy as jnp
from jax import lax
from jax.experimental import pallas as pl
from jax.experimental.pallas import tpu as pltpu
from jax.sharding import PartitionSpec as P


SOFTNESS = 0.1
EXP2_SCALE = math.log2(math.e) / SOFTNESS
EPS = 1e-6
VMEM = pl.BlockSpec(memory_space=pltpu.VMEM)
LIMIT = pltpu.CompilerParams(vmem_limit_bytes=24 << 20)
SMEM = pl.BlockSpec(memory_space=pltpu.SMEM)


def in_vmem(array):
    return pltpu.with_memory_space_constraint(array, pltpu.MemorySpace.VMEM)


def out_vmem(shape, dtype):
    return pltpu.MemorySpace.VMEM(shape, dtype)


def unit_rows(values):
    return values * lax.rsqrt(jnp.sum(values * values, axis=-1, keepdims=True) + EPS)


def project_kernel(parts, hidden_ref, proj_ref, out_ref):
    _, queries, share, embed = out_ref.shape
    projected = jnp.dot(hidden_ref[...], proj_ref[...], preferred_element_type=jnp.float32)
    projected = projected.reshape(queries, parts, share, embed)
    for part in range(parts):
        out_ref[part] = projected[:, part]


def passage_kernel(passages_ref, out_ref):
    out_ref[...] = unit_rows(passages_ref[...].astype(jnp.float32)).astype(jnp.bfloat16)


def pack_kernel(slot_ref, partial_ref, out_ref, vecs, slots):
    queries = partial_ref.shape[1]
    picks = slot_ref.shape[0] // queries
    total = partial_ref[0]
    for part in range(1, partial_ref.shape[0]):
        total = total + partial_ref[part]
    vecs[...] = unit_rows(total)
    slots[...] = jnp.zeros_like(slots)

    def place(query, carry):
        for pick in range(picks):
            slots[slot_ref[query * picks + pick]] = vecs[query]
        return carry

    lax.fori_loop(0, queries, place, 0, unroll=8)
    out_ref[...] = slots[...].reshape(out_ref.shape).astype(jnp.bfloat16)


def score_kernel(capacity, *refs):
    slots_ref, *passage_refs, out_ref, wide, turned, sums = refs
    parts = len(passage_refs)
    share, count, _, width = sums.shape
    own = count // parts
    tokens = passage_refs[0].shape[0] // own
    dp = width // capacity
    group = 8
    mine = lax.axis_index("mp")
    wide[...] = slots_ref[...].astype(jnp.float32)
    for token in range(share):
        for rank in range(capacity):
            rows = wide[pl.ds(rank * share + token, dp, stride=capacity * share), :]
            turned[token, rank * dp : (rank + 1) * dp] = rows.astype(jnp.bfloat16)

    def one_token(token, carry):
        vecs = turned[token]
        for part in range(parts):
            for first in range(0, own, group):
                sims = lax.dot_general(
                    passage_refs[part][first * tokens : (first + group) * tokens, :],
                    vecs,
                    (((1,), (1,)), ((), ())),
                    preferred_element_type=jnp.float32,
                )
                raised = jnp.exp2(sims * EXP2_SCALE)
                place = lax.rem(mine + (parts - part), parts) * own + first
                sums[token, pl.ds(place, group)] = jnp.sum(
                    raised.reshape(group, tokens // 8, 8, width), axis=1
                )
        return carry

    lax.fori_loop(0, share, one_token, 0, unroll=True)
    logs = jnp.log(jnp.sum(sums[0], axis=1))
    for token in range(1, share):
        logs = logs + jnp.log(jnp.sum(sums[token], axis=1))
    logs = logs * SOFTNESS
    stacked = jnp.concatenate(
        [logs[:, rank * dp : (rank + 1) * dp] for rank in range(capacity)], axis=0
    )
    scores = stacked.T
    for part in range(parts):
        out_ref[pl.ds(part, dp, stride=parts), :] = scores


def loss_kernel(slot_ref, partial_ref, teacher_ref, out_ref, scores, student):
    pairs, queries, width = student.shape
    count = width // 2
    dp = scores.shape[0]
    parts = partial_ref.shape[0] // dp
    total = partial_ref[pl.ds(0, dp, stride=parts), :]
    for part in range(1, parts):
        total = total + partial_ref[pl.ds(part, dp, stride=parts), :]
    scores[...] = total
    lane = lax.broadcasted_iota(jnp.int32, (1, width), 1)

    def one_query(query, carry):
        for pair in range(pairs):
            halves = []
            for half in range(2):
                slot = slot_ref[(query * pairs + pair) * 2 + half]
                values = scores[pl.ds(slot // 2, 1), :]
                turned = pltpu.roll(values, count, 1)
                halves.append(jnp.where(slot % 2 == half, values, turned))
            student[pair, pl.ds(query, 1), :] = jnp.where(lane < count, halves[0], halves[1])
        return carry

    lax.fori_loop(0, queries, one_query, 0, unroll=8)
    chosen = jnp.concatenate([student[pair] for pair in range(pairs)], axis=1)
    teacher = teacher_ref[...]
    teacher_logp = teacher - jnp.log(jnp.sum(jnp.exp(teacher), axis=1, keepdims=True))
    loss = jnp.sum(jnp.exp(teacher_logp) * (teacher_logp - chosen), axis=1, keepdims=True)
    loss = loss + jnp.log(jnp.sum(jnp.exp(chosen), axis=1, keepdims=True))
    out_ref[...] = jnp.broadcast_to(loss, (queries, 128)).T[:1]


def scored_loss(query_hidden, query_proj, passages, teacher, neg_blocks):
    dp = lax.axis_size("dp")
    mp = lax.axis_size("mp")
    queries, tokens, features = query_hidden.shape
    embed = query_proj.shape[1]
    picks = neg_blocks.shape[1]
    rows = queries * picks
    capacity = 2
    share = tokens // mp
    own_count, passage_tokens, _ = passages.shape
    count = own_count * mp

    partial = pl.pallas_call(
        functools.partial(project_kernel, mp),
        out_shape=out_vmem((mp, queries, share, embed), jnp.float32),
        in_specs=[VMEM, VMEM],
        out_specs=VMEM,
        compiler_params=LIMIT,
        name="project",
    )(query_hidden.reshape(queries * tokens, features), query_proj)
    partial = lax.all_to_all(
        partial.reshape(mp, queries * share, embed), "mp", 0, 0, tiled=True
    ).reshape(mp, queries, share, embed)

    own_vecs = pl.pallas_call(
        passage_kernel,
        out_shape=out_vmem((own_count * passage_tokens, embed), jnp.bfloat16),
        in_specs=[VMEM],
        out_specs=VMEM,
        compiler_params=LIMIT,
        name="passages",
    )(passages.reshape(own_count * passage_tokens, embed))
    passage_vecs = [own_vecs]
    for shift in range(1, mp):
        ring = [(place, (place + shift) % mp) for place in range(mp)]
        passage_vecs.append(lax.ppermute(own_vecs, "mp", ring))

    owners = neg_blocks.reshape(rows)
    row_ids = jnp.arange(rows, dtype=jnp.int32)
    earlier = (owners[:, None] == owners[None, :]) & (row_ids[None, :] < row_ids[:, None])
    ranks = jnp.sum(earlier.astype(jnp.int32), axis=1)
    slot_ids = owners * capacity + ranks
    outgoing = pl.pallas_call(
        pack_kernel,
        out_shape=out_vmem((dp, capacity * share, embed), jnp.bfloat16),
        in_specs=[SMEM, VMEM],
        out_specs=VMEM,
        scratch_shapes=[
            pltpu.VMEM((queries, share, embed), jnp.float32),
            pltpu.VMEM((dp * capacity, share, embed), jnp.float32),
        ],
        compiler_params=LIMIT,
        name="pack",
    )(slot_ids, in_vmem(partial))
    arrived = lax.all_to_all(outgoing, "dp", 0, 0, tiled=True)

    scores = pl.pallas_call(
        functools.partial(score_kernel, capacity),
        out_shape=out_vmem((dp * mp, capacity * count), jnp.float32),
        in_specs=[VMEM] * (1 + mp),
        out_specs=VMEM,
        scratch_shapes=[
            pltpu.VMEM((dp * capacity * share, embed), jnp.float32),
            pltpu.VMEM((share, dp * capacity, embed), jnp.bfloat16),
            pltpu.VMEM((share, count, 8, dp * capacity), jnp.float32),
        ],
        compiler_params=LIMIT,
        name="score",
    )(in_vmem(arrived.reshape(dp * capacity * share, embed)), *[in_vmem(v) for v in passage_vecs])
    returned = lax.all_to_all(
        scores.reshape(dp * mp, 1, capacity * count), ("dp", "mp"), 0, 0, tiled=True
    ).reshape(dp * mp, capacity * count)

    loss = pl.pallas_call(
        loss_kernel,
        out_shape=jax.ShapeDtypeStruct((1, queries), jnp.float32),
        in_specs=[SMEM, VMEM, VMEM],
        out_specs=VMEM,
        scratch_shapes=[
            pltpu.VMEM((dp, capacity * count), jnp.float32),
            pltpu.VMEM((picks // 2, queries, 2 * count), jnp.float32),
        ],
        compiler_params=LIMIT,
        name="loss",
    )(slot_ids, in_vmem(returned), teacher.reshape(queries, picks * count))
    return loss.reshape(queries)


def solution(mesh):
    in_specs = (
        P("dp", None, "mp"),
        P("mp", None),
        P(("dp", "mp"), None, None),
        P("dp", None, None),
        P("dp", None),
    )
    return jax.shard_map(
        scored_loss, mesh=mesh, in_specs=in_specs, out_specs=P("dp"), check_vma=False
    )
```

```python
import functools
import math

import jax
import jax.numpy as jnp
from jax import lax
from jax.experimental import pallas as pl
from jax.experimental.pallas import tpu as pltpu
from jax.sharding import PartitionSpec as P


SOFTNESS = 0.1
EXP2_SCALE = math.log2(math.e) / SOFTNESS
EPS = 1e-6
VMEM = pl.BlockSpec(memory_space=pltpu.VMEM)
LIMIT = pltpu.CompilerParams(vmem_limit_bytes=24 << 20)
SMEM = pl.BlockSpec(memory_space=pltpu.SMEM)


def in_vmem(array):
    return pltpu.with_memory_space_constraint(array, pltpu.MemorySpace.VMEM)


def out_vmem(shape, dtype):
    return pltpu.MemorySpace.VMEM(shape, dtype)


def unit_rows(values):
    return values * lax.rsqrt(jnp.sum(values * values, axis=-1, keepdims=True) + EPS)


def project_kernel(parts, hidden_ref, proj_ref, out_ref):
    _, queries, share, embed = out_ref.shape
    projected = jnp.dot(hidden_ref[...], proj_ref[...], preferred_element_type=jnp.float32)
    projected = projected.reshape(queries, parts, share, embed)
    for part in range(parts):
        out_ref[part] = projected[:, part]


def passage_kernel(passages_ref, out_ref):
    out_ref[...] = unit_rows(passages_ref[...].astype(jnp.float32)).astype(jnp.bfloat16)


def pack_kernel(slot_ref, partial_ref, out_ref, vecs, slots):
    queries = partial_ref.shape[1]
    picks = slot_ref.shape[0] // queries
    total = partial_ref[0]
    for part in range(1, partial_ref.shape[0]):
        total = total + partial_ref[part]
    vecs[...] = unit_rows(total)
    slots[...] = jnp.zeros_like(slots)

    def place(query, carry):
        for pick in range(picks):
            slots[slot_ref[query * picks + pick]] = vecs[query]
        return carry

    lax.fori_loop(0, queries, place, 0, unroll=8)
    out_ref[...] = slots[...].reshape(out_ref.shape).astype(jnp.bfloat16)


def score_kernel(capacity, *refs):
    slots_ref, *passage_refs, out_ref, wide, turned, sums = refs
    parts = len(passage_refs)
    share, count, _, width = sums.shape
    own = count // parts
    tokens = passage_refs[0].shape[0] // own
    dp = width // capacity
    group = 8
    mine = lax.axis_index("mp")
    wide[...] = slots_ref[...].astype(jnp.float32)
    for token in range(share):
        for rank in range(capacity):
            rows = wide[pl.ds(rank * share + token, dp, stride=capacity * share), :]
            turned[token, rank * dp : (rank + 1) * dp] = rows.astype(jnp.bfloat16)

    def one_token(token, carry):
        vecs = turned[token]
        for part in range(parts):
            for first in range(0, own, group):
                sims = lax.dot_general(
                    passage_refs[part][first * tokens : (first + group) * tokens, :],
                    vecs,
                    (((1,), (1,)), ((), ())),
                    preferred_element_type=jnp.float32,
                )
                raised = jnp.exp2(sims * EXP2_SCALE)
                place = lax.rem(mine + (parts - part), parts) * own + first
                sums[token, pl.ds(place, group)] = jnp.sum(
                    raised.reshape(group, tokens // 8, 8, width), axis=1
                )
        return carry

    lax.fori_loop(0, share, one_token, 0, unroll=True)
    logs = jnp.log(jnp.sum(sums[0], axis=1))
    for token in range(1, share):
        logs = logs + jnp.log(jnp.sum(sums[token], axis=1))
    logs = logs * SOFTNESS
    stacked = jnp.concatenate(
        [logs[:, rank * dp : (rank + 1) * dp] for rank in range(capacity)], axis=0
    )
    scores = stacked.T
    for part in range(parts):
        out_ref[pl.ds(part, dp, stride=parts), :] = scores


def loss_kernel(slot_ref, partial_ref, teacher_ref, out_ref, scores, student):
    pairs, queries, width = student.shape
    count = width // 2
    dp = scores.shape[0]
    parts = partial_ref.shape[0] // dp
    total = partial_ref[pl.ds(0, dp, stride=parts), :]
    for part in range(1, parts):
        total = total + partial_ref[pl.ds(part, dp, stride=parts), :]
    scores[...] = total
    lane = lax.broadcasted_iota(jnp.int32, (1, width), 1)

    def one_query(query, carry):
        for pair in range(pairs):
            halves = []
            for half in range(2):
                slot = slot_ref[(query * pairs + pair) * 2 + half]
                values = scores[pl.ds(slot // 2, 1), :]
                turned = pltpu.roll(values, count, 1)
                halves.append(jnp.where(slot % 2 == half, values, turned))
            student[pair, pl.ds(query, 1), :] = jnp.where(lane < count, halves[0], halves[1])
        return carry

    lax.fori_loop(0, queries, one_query, 0, unroll=8)
    chosen = jnp.concatenate([student[pair] for pair in range(pairs)], axis=1)
    teacher = teacher_ref[...]
    teacher_logp = teacher - jnp.log(jnp.sum(jnp.exp(teacher), axis=1, keepdims=True))
    loss = jnp.sum(jnp.exp(teacher_logp) * (teacher_logp - chosen), axis=1, keepdims=True)
    loss = loss + jnp.log(jnp.sum(jnp.exp(chosen), axis=1, keepdims=True))
    out_ref[...] = jnp.broadcast_to(loss, (queries, 128)).T[:1]


def scored_loss(query_hidden, query_proj, passages, teacher, neg_blocks):
    dp = lax.axis_size("dp")
    mp = lax.axis_size("mp")
    queries, tokens, features = query_hidden.shape
    embed = query_proj.shape[1]
    picks = neg_blocks.shape[1]
    rows = queries * picks
    capacity = 2
    share = tokens // mp
    own_count, passage_tokens, _ = passages.shape
    count = own_count * mp

    partial = pl.pallas_call(
        functools.partial(project_kernel, mp),
        out_shape=out_vmem((mp, queries, share, embed), jnp.float32),
        in_specs=[VMEM, VMEM],
        out_specs=VMEM,
        name="project",
    )(query_hidden.reshape(queries * tokens, features), query_proj)
    partial = lax.all_to_all(
        partial.reshape(mp, queries * share, embed), "mp", 0, 0, tiled=True
    ).reshape(mp, queries, share, embed)

    own_vecs = pl.pallas_call(
        passage_kernel,
        out_shape=out_vmem((own_count * passage_tokens, embed), jnp.bfloat16),
        in_specs=[VMEM],
        out_specs=VMEM,
        compiler_params=LIMIT,
        name="passages",
    )(passages.reshape(own_count * passage_tokens, embed))
    up = [(place, (place + 1) % mp) for place in range(mp)]
    down = [(place, (place + mp - 1) % mp) for place in range(mp)]
    below = lax.ppermute(own_vecs, "mp", up)
    above = lax.ppermute(own_vecs, "mp", down)
    opposite = lax.ppermute(below, "mp", up)
    passage_vecs = [own_vecs, below, opposite, above]

    owners = neg_blocks.reshape(rows)
    row_ids = jnp.arange(rows, dtype=jnp.int32)
    earlier = (owners[:, None] == owners[None, :]) & (row_ids[None, :] < row_ids[:, None])
    ranks = jnp.sum(earlier.astype(jnp.int32), axis=1)
    slot_ids = owners * capacity + ranks
    outgoing = pl.pallas_call(
        pack_kernel,
        out_shape=out_vmem((dp, capacity * share, embed), jnp.bfloat16),
        in_specs=[SMEM, VMEM],
        out_specs=VMEM,
        scratch_shapes=[
            pltpu.VMEM((queries, share, embed), jnp.float32),
            pltpu.VMEM((dp * capacity, share, embed), jnp.float32),
        ],
        compiler_params=LIMIT,
        name="pack",
    )(slot_ids, in_vmem(partial))
    arrived = lax.all_to_all(outgoing, "dp", 0, 0, tiled=True)

    scores = pl.pallas_call(
        functools.partial(score_kernel, capacity),
        out_shape=out_vmem((dp * mp, capacity * count), jnp.float32),
        in_specs=[VMEM] * (1 + mp),
        out_specs=VMEM,
        scratch_shapes=[
            pltpu.VMEM((dp * capacity * share, embed), jnp.float32),
            pltpu.VMEM((share, dp * capacity, embed), jnp.bfloat16),
            pltpu.VMEM((share, count, 8, dp * capacity), jnp.float32),
        ],
        compiler_params=LIMIT,
        name="score",
    )(in_vmem(arrived.reshape(dp * capacity * share, embed)), *[in_vmem(v) for v in passage_vecs])
    returned = lax.all_to_all(
        scores.reshape(dp * mp, 1, capacity * count), ("dp", "mp"), 0, 0, tiled=True
    ).reshape(dp * mp, capacity * count)

    loss = pl.pallas_call(
        loss_kernel,
        out_shape=jax.ShapeDtypeStruct((1, queries), jnp.float32),
        in_specs=[SMEM, VMEM, VMEM],
        out_specs=VMEM,
        scratch_shapes=[
            pltpu.VMEM((dp, capacity * count), jnp.float32),
            pltpu.VMEM((picks // 2, queries, 2 * count), jnp.float32),
        ],
        compiler_params=LIMIT,
        name="loss",
    )(slot_ids, in_vmem(returned), teacher.reshape(queries, picks * count))
    return loss.reshape(queries)


def solution(mesh):
    in_specs = (
        P("dp", None, "mp"),
        P("mp", None),
        P(("dp", "mp"), None, None),
        P("dp", None, None),
        P("dp", None),
    )
    return jax.shard_map(
        scored_loss, mesh=mesh, in_specs=in_specs, out_specs=P("dp"), check_vma=False
    )
```

```python
import functools
import math

import jax
import jax.numpy as jnp
from jax import lax
from jax.experimental import pallas as pl
from jax.experimental.pallas import tpu as pltpu
from jax.sharding import PartitionSpec as P


SOFTNESS = 0.1
EXP2_SCALE = math.log2(math.e) / SOFTNESS
EPS = 1e-6
VMEM = pl.BlockSpec(memory_space=pltpu.VMEM)
LIMIT = pltpu.CompilerParams(vmem_limit_bytes=24 << 20)
SMEM = pl.BlockSpec(memory_space=pltpu.SMEM)


def in_vmem(array):
    return pltpu.with_memory_space_constraint(array, pltpu.MemorySpace.VMEM)


def out_vmem(shape, dtype):
    return pltpu.MemorySpace.VMEM(shape, dtype)


def unit_rows(values):
    return values * lax.rsqrt(jnp.sum(values * values, axis=-1, keepdims=True) + EPS)


def project_kernel(hidden_ref, proj_ref, out_ref):
    parts, queries, share, embed = out_ref.shape
    projected = jnp.dot(hidden_ref[...], proj_ref[...], preferred_element_type=jnp.float32)
    projected = projected.reshape(queries, parts, share, embed)
    for part in range(parts):
        out_ref[part] = projected[:, part].astype(out_ref.dtype)


def passage_kernel(passages_ref, out_ref):
    out_ref[...] = unit_rows(passages_ref[...].astype(jnp.float32)).astype(jnp.bfloat16)


def pack_kernel(slot_ref, partial_ref, out_ref, vecs, slots):
    queries = partial_ref.shape[1]
    picks = slot_ref.shape[0] // queries
    total = partial_ref[0].astype(jnp.float32)
    for part in range(1, partial_ref.shape[0]):
        total = total + partial_ref[part].astype(jnp.float32)
    vecs[...] = unit_rows(total)
    slots[...] = jnp.zeros_like(slots)

    def place(query, carry):
        for pick in range(picks):
            slots[slot_ref[query * picks + pick]] = vecs[query]
        return carry

    lax.fori_loop(0, queries, place, 0, unroll=8)
    out_ref[...] = slots[...].reshape(out_ref.shape).astype(jnp.bfloat16)


def soft_sums(turned, passage_refs, sums):
    share, count, _, width = sums.shape
    own = count // len(passage_refs)
    tokens = passage_refs[0].shape[0] // own
    group = 8

    def one_token(token, carry):
        vecs = turned[token]
        for part, passage_ref in enumerate(passage_refs):
            for first in range(0, own, group):
                sims = lax.dot_general(
                    passage_ref[first * tokens : (first + group) * tokens, :],
                    vecs,
                    (((1,), (1,)), ((), ())),
                    preferred_element_type=jnp.float32,
                )
                raised = jnp.exp2(sims * EXP2_SCALE)
                place = part * own + first
                sums[token, place : place + group] = jnp.sum(
                    raised.reshape(group, tokens // 8, 8, width), axis=1
                )
        return carry

    lax.fori_loop(0, share, one_token, 0, unroll=True)
    logs = jnp.log(jnp.sum(sums[0], axis=1))
    for token in range(1, share):
        logs = logs + jnp.log(jnp.sum(sums[token], axis=1))
    return logs * SOFTNESS


def near_kernel(capacity, slots_ref, own_ref, below_ref, turned_ref, out_ref, wide, sums):
    share, width, _ = turned_ref.shape
    dp = width // capacity
    wide[...] = slots_ref[...].astype(jnp.float32)
    for token in range(share):
        for rank in range(capacity):
            rows = wide[pl.ds(rank * share + token, dp, stride=capacity * share), :]
            turned_ref[token, rank * dp : (rank + 1) * dp] = rows.astype(jnp.bfloat16)
    out_ref[...] = soft_sums(turned_ref, [own_ref, below_ref], sums)


def far_kernel(capacity, turned_ref, opposite_ref, above_ref, near_ref, out_ref, ordered, sums):
    parts = 4
    count, width = ordered.shape
    own = count // parts
    dp = width // capacity
    far = soft_sums(turned_ref, [opposite_ref, above_ref], sums)
    mine = lax.axis_index("mp")
    blocks = [near_ref[:own], near_ref[own:], far[:own], far[own:]]
    for below, block in enumerate(blocks):
        place = pl.multiple_of(lax.rem(mine + (parts - below), parts) * own, own)
        ordered[pl.ds(place, own), :] = block
    scores = jnp.concatenate(
        [ordered[:, rank * dp : (rank + 1) * dp] for rank in range(capacity)], axis=0
    ).T
    for part in range(parts):
        out_ref[pl.ds(part, dp, stride=parts), :] = scores


def loss_kernel(slot_ref, partial_ref, teacher_ref, out_ref, student):
    rows, count = student.shape
    queries = out_ref.shape[1]
    picks = rows // queries
    capacity = partial_ref.shape[1] // count
    dp = 128
    parts = partial_ref.shape[0] // dp
    total = partial_ref[pl.ds(0, dp, stride=parts), :]
    for part in range(1, parts):
        total = total + partial_ref[pl.ds(part, dp, stride=parts), :]
    table = jnp.concatenate(
        [total[:, rank * count : (rank + 1) * count] for rank in range(capacity)], axis=0
    )
    slots = slot_ref[...]
    places = lax.rem(slots, capacity) * dp + lax.div(slots, capacity)
    chosen = lax.broadcasted_iota(jnp.int32, (capacity * dp, rows), 0) == places
    student[...] = lax.dot_general(
        chosen.astype(jnp.float32),
        table,
        (((0,), (0,)), ((), ())),
        precision=lax.Precision.HIGHEST,
        preferred_element_type=jnp.float32,
    )
    teachers = [teacher_ref[pl.ds(pick, queries, stride=picks), :] for pick in range(picks)]
    students = [student[pl.ds(pick, queries, stride=picks), :] for pick in range(picks)]
    raised = sum(jnp.exp(scores) for scores in teachers)
    log_total = jnp.log(jnp.sum(raised, axis=1, keepdims=True))
    terms = 0.0
    for scores, guesses in zip(teachers, students):
        logp = scores - log_total
        terms = terms + jnp.exp(logp) * (logp - guesses)
    raised = sum(jnp.exp(guesses) for guesses in students)
    loss = jnp.sum(terms, axis=1, keepdims=True) + jnp.log(
        jnp.sum(raised, axis=1, keepdims=True)
    )
    out_ref[...] = jnp.broadcast_to(loss, (queries, 128)).T[:1]


def scored_loss(query_hidden, query_proj, passages, teacher, neg_blocks):
    dp = lax.axis_size("dp")
    mp = lax.axis_size("mp")
    queries, tokens, features = query_hidden.shape
    embed = query_proj.shape[1]
    picks = neg_blocks.shape[1]
    rows = queries * picks
    capacity = 2
    share = tokens // mp
    own_count, passage_tokens, _ = passages.shape
    count = own_count * mp

    steps = 4
    partial = pl.pallas_call(
        project_kernel,
        grid=(steps,),
        out_shape=jax.ShapeDtypeStruct((mp, queries, share, embed), jnp.bfloat16),
        in_specs=[
            pl.BlockSpec((queries * tokens // steps, features), lambda step: (step, 0)),
            pl.BlockSpec((features, embed), lambda step: (0, 0)),
        ],
        out_specs=pl.BlockSpec((mp, queries // steps, share, embed), lambda step: (0, step, 0, 0)),
        name="project",
    )(query_hidden.reshape(queries * tokens, features), query_proj)
    partial = lax.all_to_all(
        partial.reshape(mp, queries * share, embed), "mp", 0, 0, tiled=True
    ).reshape(mp, queries, share, embed)

    own_vecs = pl.pallas_call(
        passage_kernel,
        out_shape=out_vmem((own_count * passage_tokens, embed), jnp.bfloat16),
        in_specs=[VMEM],
        out_specs=VMEM,
        compiler_params=LIMIT,
        name="passages",
    )(passages.reshape(own_count * passage_tokens, embed))
    up = [(place, (place + 1) % mp) for place in range(mp)]
    down = [(place, (place + mp - 1) % mp) for place in range(mp)]
    below = lax.ppermute(own_vecs, "mp", up)
    above = lax.ppermute(own_vecs, "mp", down)
    opposite = lax.ppermute(below, "mp", up)

    owners = neg_blocks.reshape(rows)
    row_ids = jnp.arange(rows, dtype=jnp.int32)
    earlier = (owners[:, None] == owners[None, :]) & (row_ids[None, :] < row_ids[:, None])
    ranks = jnp.sum(earlier.astype(jnp.int32), axis=1)
    slot_ids = owners * capacity + ranks
    outgoing = pl.pallas_call(
        pack_kernel,
        out_shape=out_vmem((dp, capacity * share, embed), jnp.bfloat16),
        in_specs=[SMEM, VMEM],
        out_specs=VMEM,
        scratch_shapes=[
            pltpu.VMEM((queries, share, embed), jnp.float32),
            pltpu.VMEM((dp * capacity, share, embed), jnp.float32),
        ],
        compiler_params=LIMIT,
        name="pack",
    )(slot_ids, in_vmem(partial))
    arrived = lax.all_to_all(outgoing, "dp", 0, 0, tiled=True)

    turned, near = pl.pallas_call(
        functools.partial(near_kernel, capacity),
        out_shape=[
            out_vmem((share, capacity * dp, embed), jnp.bfloat16),
            out_vmem((count // 2, capacity * dp), jnp.float32),
        ],
        in_specs=[VMEM] * 3,
        out_specs=[VMEM] * 2,
        scratch_shapes=[
            pltpu.VMEM((dp * capacity * share, embed), jnp.float32),
            pltpu.VMEM((share, count // 2, 8, dp * capacity), jnp.float32),
        ],
        compiler_params=LIMIT,
        name="score_near",
    )(in_vmem(arrived.reshape(dp * capacity * share, embed)), in_vmem(own_vecs), in_vmem(below))
    scores = pl.pallas_call(
        functools.partial(far_kernel, capacity),
        out_shape=jax.ShapeDtypeStruct((dp * mp, capacity * count), jnp.float32),
        in_specs=[VMEM] * 4,
        out_specs=VMEM,
        scratch_shapes=[
            pltpu.VMEM((count, capacity * dp), jnp.float32),
            pltpu.VMEM((share, count // 2, 8, dp * capacity), jnp.float32),
        ],
        compiler_params=LIMIT,
        name="score_far",
    )(in_vmem(turned), in_vmem(opposite), in_vmem(above), in_vmem(near))
    returned = lax.all_to_all(
        scores.reshape(dp * mp, 1, capacity * count), ("dp", "mp"), 0, 0, tiled=True
    ).reshape(dp * mp, capacity * count)

    loss = pl.pallas_call(
        loss_kernel,
        out_shape=jax.ShapeDtypeStruct((1, queries), jnp.float32),
        in_specs=[VMEM] * 3,
        out_specs=VMEM,
        scratch_shapes=[pltpu.VMEM((rows, count), jnp.float32)],
        compiler_params=LIMIT,
        name="loss",
    )(slot_ids.reshape(1, rows), in_vmem(returned), teacher.reshape(rows, count))
    return loss.reshape(queries)


def solution(mesh):
    in_specs = (
        P("dp", None, "mp"),
        P("mp", None),
        P(("dp", "mp"), None, None),
        P("dp", None, None),
        P("dp", None),
    )
    return jax.shard_map(
        scored_loss, mesh=mesh, in_specs=in_specs, out_specs=P("dp"), check_vma=False
    )
```

```python
import functools
import math

import jax
import jax.numpy as jnp
from jax import lax
from jax.experimental import pallas as pl
from jax.experimental.pallas import tpu as pltpu
from jax.sharding import PartitionSpec as P


SOFTNESS = 0.1
EXP2_SCALE = math.log2(math.e) / SOFTNESS
EPS = 1e-6
VMEM = pl.BlockSpec(memory_space=pltpu.VMEM)
LIMIT = pltpu.CompilerParams(vmem_limit_bytes=24 << 20)
SMEM = pl.BlockSpec(memory_space=pltpu.SMEM)


def in_vmem(array):
    return pltpu.with_memory_space_constraint(array, pltpu.MemorySpace.VMEM)


def out_vmem(shape, dtype):
    return pltpu.MemorySpace.VMEM(shape, dtype)


def unit_rows(values):
    return values * lax.rsqrt(jnp.sum(values * values, axis=-1, keepdims=True) + EPS)


def project_kernel(hidden_ref, proj_ref, out_ref):
    parts, queries, share, embed = out_ref.shape
    projected = jnp.dot(hidden_ref[...], proj_ref[...], preferred_element_type=jnp.float32)
    projected = projected.reshape(queries, parts, share, embed)
    for part in range(parts):
        out_ref[part] = projected[:, part].astype(out_ref.dtype)


def passage_kernel(passages_ref, out_ref):
    out_ref[...] = unit_rows(passages_ref[...].astype(jnp.float32)).astype(jnp.bfloat16)


def pack_kernel(slot_ref, partial_ref, out_ref, vecs, slots):
    queries = partial_ref.shape[1]
    picks = slot_ref.shape[0] // queries
    total = partial_ref[0].astype(jnp.float32)
    for part in range(1, partial_ref.shape[0]):
        total = total + partial_ref[part].astype(jnp.float32)
    vecs[...] = unit_rows(total)
    slots[...] = jnp.zeros_like(slots)

    def place(query, carry):
        for pick in range(picks):
            slots[slot_ref[query * picks + pick]] = vecs[query]
        return carry

    lax.fori_loop(0, queries, place, 0, unroll=8)
    out_ref[...] = slots[...].reshape(out_ref.shape).astype(jnp.bfloat16)


def soft_sums(turned, passage_refs, sums):
    share, count, _, width = sums.shape
    own = count // len(passage_refs)
    tokens = passage_refs[0].shape[0] // own
    group = 8

    def one_token(token, carry):
        vecs = turned[token]
        for part, passage_ref in enumerate(passage_refs):
            for first in range(0, own, group):
                sims = lax.dot_general(
                    passage_ref[first * tokens : (first + group) * tokens, :],
                    vecs,
                    (((1,), (1,)), ((), ())),
                    preferred_element_type=jnp.float32,
                )
                raised = jnp.exp2(sims * EXP2_SCALE)
                place = part * own + first
                sums[token, place : place + group] = jnp.sum(
                    raised.reshape(group, tokens // 8, 8, width), axis=1
                )
        return carry

    lax.fori_loop(0, share, one_token, 0, unroll=True)
    logs = jnp.log(jnp.sum(sums[0], axis=1))
    for token in range(1, share):
        logs = logs + jnp.log(jnp.sum(sums[token], axis=1))
    return logs * SOFTNESS


def near_kernel(capacity, slots_ref, own_ref, below_ref, turned_ref, out_ref, wide, sums):
    share, width, _ = turned_ref.shape
    dp = width // capacity
    wide[...] = slots_ref[...].astype(jnp.float32)
    for token in range(share):
        for rank in range(capacity):
            rows = wide[pl.ds(rank * share + token, dp, stride=capacity * share), :]
            turned_ref[token, rank * dp : (rank + 1) * dp] = rows.astype(jnp.bfloat16)
    out_ref[...] = soft_sums(turned_ref, [own_ref, below_ref], sums)


def far_kernel(capacity, turned_ref, opposite_ref, above_ref, near_ref, out_ref, ordered, sums):
    parts = 4
    count, width = ordered.shape
    own = count // parts
    dp = width // capacity
    far = soft_sums(turned_ref, [opposite_ref, above_ref], sums)
    mine = lax.axis_index("mp")
    blocks = [near_ref[:own], near_ref[own:], far[:own], far[own:]]
    for below, block in enumerate(blocks):
        place = pl.multiple_of(lax.rem(mine + (parts - below), parts) * own, own)
        ordered[pl.ds(place, own), :] = block
    scores = jnp.concatenate(
        [ordered[:, rank * dp : (rank + 1) * dp] for rank in range(capacity)], axis=0
    ).T
    for part in range(parts):
        out_ref[pl.ds(part, dp, stride=parts), :] = scores


def loss_kernel(slot_ref, partial_ref, teacher_ref, out_ref, student):
    rows, count = student.shape
    queries = out_ref.shape[1]
    picks = rows // queries
    capacity = partial_ref.shape[1] // count
    dp = 128
    parts = partial_ref.shape[0] // dp
    total = partial_ref[pl.ds(0, dp, stride=parts), :]
    for part in range(1, parts):
        total = total + partial_ref[pl.ds(part, dp, stride=parts), :]
    table = jnp.concatenate(
        [total[:, rank * count : (rank + 1) * count] for rank in range(capacity)], axis=0
    )
    slots = slot_ref[...]
    places = lax.rem(slots, capacity) * dp + lax.div(slots, capacity)
    chosen = lax.broadcasted_iota(jnp.int32, (capacity * dp, rows), 0) == places
    student[...] = lax.dot_general(
        chosen.astype(jnp.float32),
        table,
        (((0,), (0,)), ((), ())),
        precision=lax.Precision.HIGHEST,
        preferred_element_type=jnp.float32,
    )
    teachers = [teacher_ref[pl.ds(pick, queries, stride=picks), :] for pick in range(picks)]
    students = [student[pl.ds(pick, queries, stride=picks), :] for pick in range(picks)]
    raised = sum(jnp.exp(scores) for scores in teachers)
    log_total = jnp.log(jnp.sum(raised, axis=1, keepdims=True))
    terms = 0.0
    for scores, guesses in zip(teachers, students):
        logp = scores - log_total
        terms = terms + jnp.exp(logp) * (logp - guesses)
    raised = sum(jnp.exp(guesses) for guesses in students)
    loss = jnp.sum(terms, axis=1, keepdims=True) + jnp.log(
        jnp.sum(raised, axis=1, keepdims=True)
    )
    out_ref[...] = jnp.broadcast_to(loss, (queries, 128)).T[:1]


def scored_loss(query_hidden, query_proj, passages, teacher, neg_blocks):
    dp = lax.axis_size("dp")
    mp = lax.axis_size("mp")
    queries, tokens, features = query_hidden.shape
    embed = query_proj.shape[1]
    picks = neg_blocks.shape[1]
    rows = queries * picks
    capacity = 2
    share = tokens // mp
    own_count, passage_tokens, _ = passages.shape
    count = own_count * mp

    partial = pl.pallas_call(
        project_kernel,
        out_shape=jax.ShapeDtypeStruct((mp, queries, share, embed), jnp.bfloat16),
        in_specs=[VMEM, VMEM],
        out_specs=VMEM,
        name="project",
    )(query_hidden.reshape(queries * tokens, features), query_proj)
    partial = lax.all_to_all(
        partial.reshape(mp, queries * share, embed), "mp", 0, 0, tiled=True
    ).reshape(mp, queries, share, embed)

    own_vecs = pl.pallas_call(
        passage_kernel,
        out_shape=out_vmem((own_count * passage_tokens, embed), jnp.bfloat16),
        in_specs=[VMEM],
        out_specs=VMEM,
        compiler_params=LIMIT,
        name="passages",
    )(passages.reshape(own_count * passage_tokens, embed))
    up = [(place, (place + 1) % mp) for place in range(mp)]
    down = [(place, (place + mp - 1) % mp) for place in range(mp)]
    below = lax.ppermute(own_vecs, "mp", up)
    above = lax.ppermute(own_vecs, "mp", down)
    opposite = lax.ppermute(below, "mp", up)

    owners = neg_blocks.reshape(rows)
    row_ids = jnp.arange(rows, dtype=jnp.int32)
    earlier = (owners[:, None] == owners[None, :]) & (row_ids[None, :] < row_ids[:, None])
    ranks = jnp.sum(earlier.astype(jnp.int32), axis=1)
    slot_ids = owners * capacity + ranks
    outgoing = pl.pallas_call(
        pack_kernel,
        out_shape=out_vmem((dp, capacity * share, embed), jnp.bfloat16),
        in_specs=[SMEM, VMEM],
        out_specs=VMEM,
        scratch_shapes=[
            pltpu.VMEM((queries, share, embed), jnp.float32),
            pltpu.VMEM((dp * capacity, share, embed), jnp.float32),
        ],
        compiler_params=LIMIT,
        name="pack",
    )(slot_ids, in_vmem(partial))
    arrived = lax.all_to_all(outgoing, "dp", 0, 0, tiled=True)

    turned, near = pl.pallas_call(
        functools.partial(near_kernel, capacity),
        out_shape=[
            out_vmem((share, capacity * dp, embed), jnp.bfloat16),
            out_vmem((count // 2, capacity * dp), jnp.float32),
        ],
        in_specs=[VMEM] * 3,
        out_specs=[VMEM] * 2,
        scratch_shapes=[
            pltpu.VMEM((dp * capacity * share, embed), jnp.float32),
            pltpu.VMEM((share, count // 2, 8, dp * capacity), jnp.float32),
        ],
        compiler_params=LIMIT,
        name="score_near",
    )(in_vmem(arrived.reshape(dp * capacity * share, embed)), in_vmem(own_vecs), in_vmem(below))
    scores = pl.pallas_call(
        functools.partial(far_kernel, capacity),
        out_shape=jax.ShapeDtypeStruct((dp * mp, capacity * count), jnp.float32),
        in_specs=[VMEM] * 4,
        out_specs=VMEM,
        scratch_shapes=[
            pltpu.VMEM((count, capacity * dp), jnp.float32),
            pltpu.VMEM((share, count // 2, 8, dp * capacity), jnp.float32),
        ],
        compiler_params=LIMIT,
        name="score_far",
    )(in_vmem(turned), in_vmem(opposite), in_vmem(above), in_vmem(near))
    returned = lax.all_to_all(
        scores.reshape(dp * mp, 1, capacity * count), ("dp", "mp"), 0, 0, tiled=True
    ).reshape(dp * mp, capacity * count)

    loss = pl.pallas_call(
        loss_kernel,
        out_shape=jax.ShapeDtypeStruct((1, queries), jnp.float32),
        in_specs=[VMEM] * 3,
        out_specs=VMEM,
        scratch_shapes=[pltpu.VMEM((rows, count), jnp.float32)],
        compiler_params=LIMIT,
        name="loss",
    )(slot_ids.reshape(1, rows), in_vmem(returned), teacher.reshape(rows, count))
    return loss.reshape(queries)


def solution(mesh):
    in_specs = (
        P("dp", None, "mp"),
        P("mp", None),
        P(("dp", "mp"), None, None),
        P("dp", None, None),
        P("dp", None),
    )
    return jax.shard_map(
        scored_loss, mesh=mesh, in_specs=in_specs, out_specs=P("dp"), check_vma=False
    )
```

```python
import functools
import math

import jax
import jax.numpy as jnp
from jax import lax
from jax.experimental import pallas as pl
from jax.experimental.pallas import tpu as pltpu
from jax.sharding import PartitionSpec as P


SOFTNESS = 0.1
EXP2_SCALE = math.log2(math.e) / SOFTNESS
EPS = 1e-6
VMEM = pl.BlockSpec(memory_space=pltpu.VMEM)
LIMIT = pltpu.CompilerParams(vmem_limit_bytes=24 << 20)
ANY = pl.BlockSpec(memory_space=pl.ANY)
SMEM = pl.BlockSpec(memory_space=pltpu.SMEM)


def in_vmem(array):
    return pltpu.with_memory_space_constraint(array, pltpu.MemorySpace.VMEM)


def out_vmem(shape, dtype):
    return pltpu.MemorySpace.VMEM(shape, dtype)


def unit_rows(values):
    return values * lax.rsqrt(jnp.sum(values * values, axis=-1, keepdims=True) + EPS)


def project_kernel(hidden_ref, proj_ref, out_ref, hidden, proj, projected, arrivals, leaves, ready):
    parts, queries, share, embed = out_ref.shape
    steps = arrivals.shape[0]
    rows = hidden.shape[0] // steps
    some = queries // steps

    def arrival(step):
        block = pl.ds(step * rows, rows)
        return pltpu.make_async_copy(hidden_ref.at[block], hidden.at[block], arrivals.at[step])

    def leave(step):
        block = pl.ds(step * some, some)
        return pltpu.make_async_copy(
            projected.at[:, block], out_ref.at[:, block], leaves.at[step]
        )

    whole = pltpu.make_async_copy(proj_ref, proj, ready)
    whole.start()
    for step in range(steps):
        arrival(step).start()
    whole.wait()
    for step in range(steps):
        arrival(step).wait()
        block = jnp.dot(
            hidden[step * rows : (step + 1) * rows],
            proj[...],
            preferred_element_type=jnp.float32,
        ).reshape(some, parts, share, embed)
        for part in range(parts):
            projected[part, step * some : (step + 1) * some] = block[:, part].astype(
                projected.dtype
            )
        leave(step).start()
    for step in range(steps):
        leave(step).wait()


def passage_kernel(passages_ref, out_ref):
    out_ref[...] = unit_rows(passages_ref[...].astype(jnp.float32)).astype(jnp.bfloat16)


def pack_kernel(slot_ref, partial_ref, out_ref, vecs, slots, packed, leaves):
    queries = partial_ref.shape[1]
    picks = slot_ref.shape[0] // queries
    total = partial_ref[0].astype(jnp.float32)
    for part in range(1, partial_ref.shape[0]):
        total = total + partial_ref[part].astype(jnp.float32)
    vecs[...] = unit_rows(total)
    slots[...] = jnp.zeros_like(slots)

    def place(query, carry):
        for pick in range(picks):
            slots[slot_ref[query * picks + pick]] = vecs[query]
        return carry

    lax.fori_loop(0, queries, place, 0, unroll=8)
    steps = leaves.shape[0]
    owners = packed.shape[0] // steps
    per_step = slots.shape[0] // steps

    def leave(step):
        block = pl.ds(step * owners, owners)
        return pltpu.make_async_copy(packed.at[block], out_ref.at[block], leaves.at[step])

    for step in range(steps):
        packed[step * owners : (step + 1) * owners] = (
            slots[step * per_step : (step + 1) * per_step]
            .reshape(owners, *packed.shape[1:])
            .astype(jnp.bfloat16)
        )
        leave(step).start()
    for step in range(steps):
        leave(step).wait()


def soft_sums(turned, passage_refs, sums):
    share, count, _, width = sums.shape
    own = count // len(passage_refs)
    tokens = passage_refs[0].shape[0] // own
    group = 8

    def one_token(token, carry):
        vecs = turned[token]
        for part, passage_ref in enumerate(passage_refs):
            for first in range(0, own, group):
                sims = lax.dot_general(
                    passage_ref[first * tokens : (first + group) * tokens, :],
                    vecs,
                    (((1,), (1,)), ((), ())),
                    preferred_element_type=jnp.float32,
                )
                raised = jnp.exp2(sims * EXP2_SCALE)
                place = part * own + first
                sums[token, place : place + group] = jnp.sum(
                    raised.reshape(group, tokens // 8, 8, width), axis=1
                )
        return carry

    lax.fori_loop(0, share, one_token, 0, unroll=True)
    logs = jnp.log(jnp.sum(sums[0], axis=1))
    for token in range(1, share):
        logs = logs + jnp.log(jnp.sum(sums[token], axis=1))
    return logs * SOFTNESS


def near_kernel(capacity, slots_ref, own_ref, below_ref, turned_ref, out_ref, wide, sums):
    share, width, _ = turned_ref.shape
    dp = width // capacity
    wide[...] = slots_ref[...].astype(jnp.float32)
    for token in range(share):
        for rank in range(capacity):
            rows = wide[pl.ds(rank * share + token, dp, stride=capacity * share), :]
            turned_ref[token, rank * dp : (rank + 1) * dp] = rows.astype(jnp.bfloat16)
    out_ref[...] = soft_sums(turned_ref, [own_ref, below_ref], sums)


def far_kernel(capacity, turned_ref, opposite_ref, above_ref, near_ref, out_ref, ordered, sums):
    parts = 4
    count, width = ordered.shape
    own = count // parts
    dp = width // capacity
    far = soft_sums(turned_ref, [opposite_ref, above_ref], sums)
    mine = lax.axis_index("mp")
    blocks = [near_ref[:own], near_ref[own:], far[:own], far[own:]]
    for below, block in enumerate(blocks):
        place = pl.multiple_of(lax.rem(mine + (parts - below), parts) * own, own)
        ordered[pl.ds(place, own), :] = block
    scores = jnp.concatenate(
        [ordered[:, rank * dp : (rank + 1) * dp] for rank in range(capacity)], axis=0
    ).T
    for part in range(parts):
        out_ref[pl.ds(part, dp, stride=parts), :] = scores


def loss_kernel(slot_ref, partial_ref, teacher_ref, out_ref, student):
    rows, count = student.shape
    queries = out_ref.shape[1]
    picks = rows // queries
    capacity = partial_ref.shape[1] // count
    dp = 128
    parts = partial_ref.shape[0] // dp
    total = partial_ref[pl.ds(0, dp, stride=parts), :]
    for part in range(1, parts):
        total = total + partial_ref[pl.ds(part, dp, stride=parts), :]
    table = jnp.concatenate(
        [total[:, rank * count : (rank + 1) * count] for rank in range(capacity)], axis=0
    )
    slots = slot_ref[...]
    places = lax.rem(slots, capacity) * dp + lax.div(slots, capacity)
    chosen = lax.broadcasted_iota(jnp.int32, (capacity * dp, rows), 0) == places
    student[...] = lax.dot_general(
        chosen.astype(jnp.float32),
        table,
        (((0,), (0,)), ((), ())),
        precision=lax.Precision.HIGHEST,
        preferred_element_type=jnp.float32,
    )
    teachers = [teacher_ref[pl.ds(pick, queries, stride=picks), :] for pick in range(picks)]
    students = [student[pl.ds(pick, queries, stride=picks), :] for pick in range(picks)]
    raised = sum(jnp.exp(scores) for scores in teachers)
    log_total = jnp.log(jnp.sum(raised, axis=1, keepdims=True))
    terms = 0.0
    for scores, guesses in zip(teachers, students):
        logp = scores - log_total
        terms = terms + jnp.exp(logp) * (logp - guesses)
    raised = sum(jnp.exp(guesses) for guesses in students)
    loss = jnp.sum(terms, axis=1, keepdims=True) + jnp.log(
        jnp.sum(raised, axis=1, keepdims=True)
    )
    out_ref[...] = jnp.broadcast_to(loss, (queries, 128)).T[:1]


def scored_loss(query_hidden, query_proj, passages, teacher, neg_blocks):
    dp = lax.axis_size("dp")
    mp = lax.axis_size("mp")
    queries, tokens, features = query_hidden.shape
    embed = query_proj.shape[1]
    picks = neg_blocks.shape[1]
    rows = queries * picks
    capacity = 2
    share = tokens // mp
    own_count, passage_tokens, _ = passages.shape
    count = own_count * mp

    partial = pl.pallas_call(
        project_kernel,
        out_shape=jax.ShapeDtypeStruct((mp, queries, share, embed), jnp.bfloat16),
        in_specs=[ANY, ANY],
        out_specs=ANY,
        scratch_shapes=[
            pltpu.VMEM((queries * tokens, features), jnp.bfloat16),
            pltpu.VMEM((features, embed), jnp.bfloat16),
            pltpu.VMEM((mp, queries, share, embed), jnp.bfloat16),
            pltpu.SemaphoreType.DMA((4,)),
            pltpu.SemaphoreType.DMA((4,)),
            pltpu.SemaphoreType.DMA,
        ],
        name="project",
    )(query_hidden.reshape(queries * tokens, features), query_proj)
    partial = lax.all_to_all(
        partial.reshape(mp, queries * share, embed), "mp", 0, 0, tiled=True
    ).reshape(mp, queries, share, embed)

    own_vecs = pl.pallas_call(
        passage_kernel,
        out_shape=out_vmem((own_count * passage_tokens, embed), jnp.bfloat16),
        in_specs=[VMEM],
        out_specs=VMEM,
        compiler_params=LIMIT,
        name="passages",
    )(passages.reshape(own_count * passage_tokens, embed))
    up = [(place, (place + 1) % mp) for place in range(mp)]
    down = [(place, (place + mp - 1) % mp) for place in range(mp)]
    below = lax.ppermute(own_vecs, "mp", up)
    above = lax.ppermute(own_vecs, "mp", down)
    opposite = lax.ppermute(below, "mp", up)

    owners = neg_blocks.reshape(rows)
    row_ids = jnp.arange(rows, dtype=jnp.int32)
    earlier = (owners[:, None] == owners[None, :]) & (row_ids[None, :] < row_ids[:, None])
    ranks = jnp.sum(earlier.astype(jnp.int32), axis=1)
    slot_ids = owners * capacity + ranks
    outgoing = pl.pallas_call(
        pack_kernel,
        out_shape=out_vmem((dp, capacity * share, embed), jnp.bfloat16),
        in_specs=[SMEM, VMEM],
        out_specs=ANY,
        scratch_shapes=[
            pltpu.VMEM((queries, share, embed), jnp.float32),
            pltpu.VMEM((dp * capacity, share, embed), jnp.float32),
            pltpu.VMEM((dp, capacity * share, embed), jnp.bfloat16),
            pltpu.SemaphoreType.DMA((4,)),
        ],
        compiler_params=LIMIT,
        name="pack",
    )(slot_ids, in_vmem(partial))
    arrived = lax.all_to_all(outgoing, "dp", 0, 0, tiled=True)

    turned, near = pl.pallas_call(
        functools.partial(near_kernel, capacity),
        out_shape=[
            out_vmem((share, capacity * dp, embed), jnp.bfloat16),
            out_vmem((count // 2, capacity * dp), jnp.float32),
        ],
        in_specs=[VMEM] * 3,
        out_specs=[VMEM] * 2,
        scratch_shapes=[
            pltpu.VMEM((dp * capacity * share, embed), jnp.float32),
            pltpu.VMEM((share, count // 2, 8, dp * capacity), jnp.float32),
        ],
        compiler_params=LIMIT,
        name="score_near",
    )(in_vmem(arrived.reshape(dp * capacity * share, embed)), in_vmem(own_vecs), in_vmem(below))
    scores = pl.pallas_call(
        functools.partial(far_kernel, capacity),
        out_shape=jax.ShapeDtypeStruct((dp * mp, capacity * count), jnp.float32),
        in_specs=[VMEM] * 4,
        out_specs=VMEM,
        scratch_shapes=[
            pltpu.VMEM((count, capacity * dp), jnp.float32),
            pltpu.VMEM((share, count // 2, 8, dp * capacity), jnp.float32),
        ],
        compiler_params=LIMIT,
        name="score_far",
    )(in_vmem(turned), in_vmem(opposite), in_vmem(above), in_vmem(near))
    returned = lax.all_to_all(
        scores.reshape(dp * mp, 1, capacity * count), ("dp", "mp"), 0, 0, tiled=True
    ).reshape(dp * mp, capacity * count)

    loss = pl.pallas_call(
        loss_kernel,
        out_shape=jax.ShapeDtypeStruct((1, queries), jnp.float32),
        in_specs=[VMEM] * 3,
        out_specs=VMEM,
        scratch_shapes=[pltpu.VMEM((rows, count), jnp.float32)],
        compiler_params=LIMIT,
        name="loss",
    )(slot_ids.reshape(1, rows), in_vmem(returned), teacher.reshape(rows, count))
    return loss.reshape(queries)


def solution(mesh):
    in_specs = (
        P("dp", None, "mp"),
        P("mp", None),
        P(("dp", "mp"), None, None),
        P("dp", None, None),
        P("dp", None),
    )
    return jax.shard_map(
        scored_loss, mesh=mesh, in_specs=in_specs, out_specs=P("dp"), check_vma=False
    )
```

```python
import functools
import math

import jax
import jax.numpy as jnp
from jax import lax
from jax.experimental import pallas as pl
from jax.experimental.pallas import tpu as pltpu
from jax.sharding import PartitionSpec as P


SOFTNESS = 0.1
EXP2_SCALE = math.log2(math.e) / SOFTNESS
EPS = 1e-6
VMEM = pl.BlockSpec(memory_space=pltpu.VMEM)
LIMIT = pltpu.CompilerParams(vmem_limit_bytes=24 << 20)
SMEM = pl.BlockSpec(memory_space=pltpu.SMEM)


def in_vmem(array):
    return pltpu.with_memory_space_constraint(array, pltpu.MemorySpace.VMEM)


def out_vmem(shape, dtype):
    return pltpu.MemorySpace.VMEM(shape, dtype)


def unit_rows(values):
    return values * lax.rsqrt(jnp.sum(values * values, axis=-1, keepdims=True) + EPS)


def project_kernel(hidden_ref, proj_ref, out_ref):
    parts, cores, queries, share, embed = out_ref.shape
    projected = jnp.dot(hidden_ref[...], proj_ref[...], preferred_element_type=jnp.float32)
    projected = projected.reshape(queries, parts, share, embed)
    for part in range(parts):
        block = projected[:, part].astype(out_ref.dtype)
        for core in range(cores):
            out_ref[part, core] = block


def passage_kernel(passages_ref, out_ref):
    out_ref[...] = unit_rows(passages_ref[...].astype(jnp.float32)).astype(jnp.bfloat16)


def pack_kernel(slot_ref, partial_ref, out_ref, vecs, slots):
    queries = partial_ref.shape[1]
    picks = slot_ref.shape[0] // queries
    total = partial_ref[0].astype(jnp.float32)
    for part in range(1, partial_ref.shape[0]):
        total = total + partial_ref[part].astype(jnp.float32)
    vecs[...] = unit_rows(total)
    slots[...] = jnp.zeros_like(slots)

    def place(query, carry):
        for pick in range(picks):
            slots[slot_ref[query * picks + pick]] = vecs[query]
        return carry

    lax.fori_loop(0, queries, place, 0, unroll=8)
    sent = slots.shape[0] - 1
    out_ref[...] = slots[:sent].reshape(out_ref.shape).astype(jnp.bfloat16)


def soft_sums(turned, passage_refs, sums):
    share, count, _, width = sums.shape
    own = count // len(passage_refs)
    tokens = passage_refs[0].shape[0] // own
    group = 8

    def one_token(token, carry):
        vecs = turned[token]
        for part, passage_ref in enumerate(passage_refs):
            for first in range(0, own, group):
                sims = lax.dot_general(
                    passage_ref[first * tokens : (first + group) * tokens, :],
                    vecs,
                    (((1,), (1,)), ((), ())),
                    preferred_element_type=jnp.float32,
                )
                raised = jnp.exp2(sims * EXP2_SCALE)
                place = part * own + first
                sums[token, place : place + group] = jnp.sum(
                    raised.reshape(group, tokens // 8, 8, width), axis=1
                )
        return carry

    lax.fori_loop(0, share, one_token, 0, unroll=True)
    logs = jnp.log(jnp.sum(sums[0], axis=1))
    for token in range(1, share):
        logs = logs + jnp.log(jnp.sum(sums[token], axis=1))
    return logs * SOFTNESS


def near_kernel(capacity, slots_ref, own_ref, below_ref, turned_ref, out_ref, wide, sums):
    share, width, _ = turned_ref.shape
    dp = width // capacity
    wide[...] = slots_ref[...].astype(jnp.float32)
    for token in range(share):
        for rank in range(capacity):
            rows = wide[pl.ds(rank * share + token, dp, stride=capacity * share), :]
            turned_ref[token, rank * dp : (rank + 1) * dp] = rows.astype(jnp.bfloat16)
    out_ref[...] = soft_sums(turned_ref, [own_ref, below_ref], sums)


def far_kernel(capacity, turned_ref, opposite_ref, above_ref, near_ref, out_ref, ordered, sums):
    parts = 4
    count, width = ordered.shape
    own = count // parts
    dp = width // capacity
    far = soft_sums(turned_ref, [opposite_ref, above_ref], sums)
    mine = lax.axis_index("mp")
    blocks = [near_ref[:own], near_ref[own:], far[:own], far[own:]]
    for below, block in enumerate(blocks):
        place = pl.multiple_of(lax.rem(mine + (parts - below), parts) * own, own)
        ordered[pl.ds(place, own), :] = block
    scores = jnp.concatenate(
        [ordered[:, rank * dp : (rank + 1) * dp] for rank in range(capacity)], axis=0
    ).T
    for part in range(parts):
        out_ref[pl.ds(part, dp, stride=parts), :] = scores


def loss_kernel(slot_ref, partial_ref, teacher_ref, out_ref, student):
    rows, count = student.shape
    queries = out_ref.shape[1]
    picks = rows // queries
    capacity = partial_ref.shape[1] // count
    dp = 128
    parts = partial_ref.shape[0] // dp
    total = partial_ref[pl.ds(0, dp, stride=parts), :]
    for part in range(1, parts):
        total = total + partial_ref[pl.ds(part, dp, stride=parts), :]
    table = jnp.concatenate(
        [total[:, rank * count : (rank + 1) * count] for rank in range(capacity)], axis=0
    )
    slots = slot_ref[...]
    places = lax.rem(slots, capacity) * dp + lax.div(slots, capacity)
    chosen = lax.broadcasted_iota(jnp.int32, (capacity * dp, rows), 0) == places
    student[...] = lax.dot_general(
        chosen.astype(jnp.float32),
        table,
        (((0,), (0,)), ((), ())),
        precision=lax.Precision.HIGHEST,
        preferred_element_type=jnp.float32,
    )
    teachers = [teacher_ref[pl.ds(pick, queries, stride=picks), :] for pick in range(picks)]
    students = [student[pl.ds(pick, queries, stride=picks), :] for pick in range(picks)]
    raised = sum(jnp.exp(scores) for scores in teachers)
    log_total = jnp.log(jnp.sum(raised, axis=1, keepdims=True))
    terms = 0.0
    for scores, guesses in zip(teachers, students):
        logp = scores - log_total
        terms = terms + jnp.exp(logp) * (logp - guesses)
    raised = sum(jnp.exp(guesses) for guesses in students)
    loss = jnp.sum(terms, axis=1, keepdims=True) + jnp.log(
        jnp.sum(raised, axis=1, keepdims=True)
    )
    out_ref[...] = jnp.broadcast_to(loss, (queries, 128)).T[:1]


def scored_loss(query_hidden, query_proj, passages, teacher, neg_blocks):
    dp = lax.axis_size("dp")
    mp = lax.axis_size("mp")
    queries, tokens, features = query_hidden.shape
    embed = query_proj.shape[1]
    picks = neg_blocks.shape[1]
    rows = queries * picks
    capacity = 2
    cores = 2
    chips = dp // cores
    share = tokens // mp
    own_count, passage_tokens, _ = passages.shape
    count = own_count * mp

    partial = pl.pallas_call(
        project_kernel,
        out_shape=jax.ShapeDtypeStruct((mp, cores, queries, share, embed), jnp.bfloat16),
        in_specs=[VMEM, VMEM],
        out_specs=VMEM,
        name="project",
    )(query_hidden.reshape(queries * tokens, features), query_proj)
    peers = [
        [(chip * cores + core) * mp + part for part in range(mp) for core in range(cores)]
        for chip in range(chips)
    ]
    partial = lax.all_to_all(
        partial.reshape(mp * cores, queries * share, embed),
        ("dp", "mp"),
        0,
        0,
        tiled=True,
        axis_index_groups=peers,
    ).reshape(mp, cores * queries, share, embed)

    own_vecs = pl.pallas_call(
        passage_kernel,
        out_shape=out_vmem((own_count * passage_tokens, embed), jnp.bfloat16),
        in_specs=[VMEM],
        out_specs=VMEM,
        compiler_params=LIMIT,
        name="passages",
    )(passages.reshape(own_count * passage_tokens, embed))
    up = [(place, (place + 1) % mp) for place in range(mp)]
    down = [(place, (place + mp - 1) % mp) for place in range(mp)]
    below = lax.ppermute(own_vecs, "mp", up)
    above = lax.ppermute(own_vecs, "mp", down)
    opposite = lax.ppermute(below, "mp", up)

    own_blocks = neg_blocks.reshape(rows)
    other_blocks = lax.ppermute(own_blocks, "dp", [(place, place ^ 1) for place in range(dp)])
    core = lax.rem(lax.axis_index("dp"), cores)
    owners = jnp.where(
        core == 0,
        jnp.stack([own_blocks, other_blocks]),
        jnp.stack([other_blocks, own_blocks]),
    )
    row_ids = jnp.arange(rows, dtype=jnp.int32)
    before = row_ids[None, :] < row_ids[:, None]
    earlier = (owners[:, :, None] == owners[:, None, :]) & before
    ranks = jnp.sum(earlier.astype(jnp.int32), axis=2)
    source_core = jnp.arange(cores, dtype=jnp.int32)[:, None]
    places = (owners // cores * cores + source_core) * capacity + ranks
    places = jnp.where(owners % cores == core, places, dp * capacity).reshape(cores * rows)
    own_earlier = (own_blocks[:, None] == own_blocks[None, :]) & before
    slot_ids = own_blocks * capacity + jnp.sum(own_earlier.astype(jnp.int32), axis=1)

    outgoing = pl.pallas_call(
        pack_kernel,
        out_shape=jax.ShapeDtypeStruct((chips, cores * capacity * share, embed), jnp.bfloat16),
        in_specs=[SMEM, VMEM],
        out_specs=VMEM,
        scratch_shapes=[
            pltpu.VMEM((cores * queries, share, embed), jnp.float32),
            pltpu.VMEM((dp * capacity + 1, share, embed), jnp.float32),
        ],
        compiler_params=LIMIT,
        name="pack",
    )(places, in_vmem(partial))
    same_core = [[chip * cores + core for chip in range(chips)] for core in range(cores)]
    arrived = lax.all_to_all(
        outgoing, "dp", 0, 0, tiled=True, axis_index_groups=same_core
    )

    turned, near = pl.pallas_call(
        functools.partial(near_kernel, capacity),
        out_shape=[
            out_vmem((share, capacity * dp, embed), jnp.bfloat16),
            out_vmem((count // 2, capacity * dp), jnp.float32),
        ],
        in_specs=[VMEM] * 3,
        out_specs=[VMEM] * 2,
        scratch_shapes=[
            pltpu.VMEM((dp * capacity * share, embed), jnp.float32),
            pltpu.VMEM((share, count // 2, 8, dp * capacity), jnp.float32),
        ],
        compiler_params=LIMIT,
        name="score_near",
    )(in_vmem(arrived.reshape(dp * capacity * share, embed)), in_vmem(own_vecs), in_vmem(below))
    scores = pl.pallas_call(
        functools.partial(far_kernel, capacity),
        out_shape=jax.ShapeDtypeStruct((dp * mp, capacity * count), jnp.float32),
        in_specs=[VMEM] * 4,
        out_specs=VMEM,
        scratch_shapes=[
            pltpu.VMEM((count, capacity * dp), jnp.float32),
            pltpu.VMEM((share, count // 2, 8, dp * capacity), jnp.float32),
        ],
        compiler_params=LIMIT,
        name="score_far",
    )(in_vmem(turned), in_vmem(opposite), in_vmem(above), in_vmem(near))
    returned = lax.all_to_all(
        scores.reshape(dp * mp, 1, capacity * count), ("dp", "mp"), 0, 0, tiled=True
    ).reshape(dp * mp, capacity * count)

    loss = pl.pallas_call(
        loss_kernel,
        out_shape=jax.ShapeDtypeStruct((1, queries), jnp.float32),
        in_specs=[VMEM] * 3,
        out_specs=VMEM,
        scratch_shapes=[pltpu.VMEM((rows, count), jnp.float32)],
        compiler_params=LIMIT,
        name="loss",
    )(slot_ids.reshape(1, rows), in_vmem(returned), teacher.reshape(rows, count))
    return loss.reshape(queries)


def solution(mesh):
    in_specs = (
        P("dp", None, "mp"),
        P("mp", None),
        P(("dp", "mp"), None, None),
        P("dp", None, None),
        P("dp", None),
    )
    return jax.shard_map(
        scored_loss, mesh=mesh, in_specs=in_specs, out_specs=P("dp"), check_vma=False
    )
```

```python
import functools
import math

import jax
import jax.numpy as jnp
from jax import lax
from jax.experimental import pallas as pl
from jax.experimental.pallas import tpu as pltpu
from jax.sharding import PartitionSpec as P


SOFTNESS = 0.1
EXP2_SCALE = math.log2(math.e) / SOFTNESS
EPS = 1e-6
VMEM = pl.BlockSpec(memory_space=pltpu.VMEM)
LIMIT = pltpu.CompilerParams(vmem_limit_bytes=24 << 20)
SMEM = pl.BlockSpec(memory_space=pltpu.SMEM)


def in_vmem(array):
    return pltpu.with_memory_space_constraint(array, pltpu.MemorySpace.VMEM)


def out_vmem(shape, dtype):
    return pltpu.MemorySpace.VMEM(shape, dtype)


def unit_rows(values):
    return values * lax.rsqrt(jnp.sum(values * values, axis=-1, keepdims=True) + EPS)


def project_kernel(hidden_ref, proj_ref, out_ref):
    parts, queries, share, embed = out_ref.shape
    projected = jnp.dot(hidden_ref[...], proj_ref[...], preferred_element_type=jnp.float32)
    projected = projected.reshape(queries, parts, share, embed)
    for part in range(parts):
        out_ref[part] = projected[:, part].astype(out_ref.dtype)


def passage_kernel(passages_ref, out_ref):
    out_ref[...] = unit_rows(passages_ref[...].astype(jnp.float32)).astype(jnp.bfloat16)


def pack_kernel(slot_ref, partial_ref, out_ref, vecs, slots):
    queries = partial_ref.shape[1]
    picks = slot_ref.shape[0] // queries
    total = partial_ref[0].astype(jnp.float32)
    for part in range(1, partial_ref.shape[0]):
        total = total + partial_ref[part].astype(jnp.float32)
    vecs[...] = unit_rows(total)
    slots[...] = jnp.zeros_like(slots)

    def place(query, carry):
        for pick in range(picks):
            slots[slot_ref[query * picks + pick]] = vecs[query]
        return carry

    lax.fori_loop(0, queries, place, 0, unroll=8)
    out_ref[...] = slots[...].reshape(out_ref.shape).astype(jnp.bfloat16)


def soft_sums(turned, passage_refs, sums):
    share, count, _, width = sums.shape
    own = count // len(passage_refs)
    tokens = passage_refs[0].shape[0] // own
    group = 16

    def one_token(token, carry):
        vecs = turned[token]
        for part, passage_ref in enumerate(passage_refs):
            for first in range(0, own, group):
                sims = lax.dot_general(
                    passage_ref[first * tokens : (first + group) * tokens, :],
                    vecs,
                    (((1,), (1,)), ((), ())),
                    preferred_element_type=jnp.float32,
                )
                raised = jnp.exp2(sims * EXP2_SCALE)
                place = part * own + first
                sums[token, place : place + group] = jnp.sum(
                    raised.reshape(group, tokens // 8, 8, width), axis=1
                )
        return carry

    lax.fori_loop(0, share, one_token, 0, unroll=True)
    logs = jnp.log(jnp.sum(sums[0], axis=1))
    for token in range(1, share):
        logs = logs + jnp.log(jnp.sum(sums[token], axis=1))
    return logs * SOFTNESS


def near_kernel(capacity, slots_ref, own_ref, below_ref, turned_ref, out_ref, wide, sums):
    share, width, _ = turned_ref.shape
    dp = width // capacity
    wide[...] = slots_ref[...].astype(jnp.float32)
    for token in range(share):
        for rank in range(capacity):
            rows = wide[pl.ds(rank * share + token, dp, stride=capacity * share), :]
            turned_ref[token, rank * dp : (rank + 1) * dp] = rows.astype(jnp.bfloat16)
    out_ref[...] = soft_sums(turned_ref, [own_ref, below_ref], sums)


def far_kernel(capacity, turned_ref, opposite_ref, above_ref, near_ref, out_ref, ordered, sums):
    parts = 4
    count, width = ordered.shape
    own = count // parts
    dp = width // capacity
    far = soft_sums(turned_ref, [opposite_ref, above_ref], sums)
    mine = lax.axis_index("mp")
    blocks = [near_ref[:own], near_ref[own:], far[:own], far[own:]]
    for below, block in enumerate(blocks):
        place = pl.multiple_of(lax.rem(mine + (parts - below), parts) * own, own)
        ordered[pl.ds(place, own), :] = block
    scores = jnp.concatenate(
        [ordered[:, rank * dp : (rank + 1) * dp] for rank in range(capacity)], axis=0
    ).T
    for part in range(parts):
        out_ref[pl.ds(part, dp, stride=parts), :] = scores


def loss_kernel(slot_ref, partial_ref, teacher_ref, out_ref, student):
    rows, count = student.shape
    queries = out_ref.shape[1]
    picks = rows // queries
    capacity = partial_ref.shape[1] // count
    dp = 128
    parts = partial_ref.shape[0] // dp
    total = partial_ref[pl.ds(0, dp, stride=parts), :]
    for part in range(1, parts):
        total = total + partial_ref[pl.ds(part, dp, stride=parts), :]
    table = jnp.concatenate(
        [total[:, rank * count : (rank + 1) * count] for rank in range(capacity)], axis=0
    )
    slots = slot_ref[...]
    places = lax.rem(slots, capacity) * dp + lax.div(slots, capacity)
    chosen = lax.broadcasted_iota(jnp.int32, (capacity * dp, rows), 0) == places
    student[...] = lax.dot_general(
        chosen.astype(jnp.float32),
        table,
        (((0,), (0,)), ((), ())),
        precision=lax.Precision.HIGHEST,
        preferred_element_type=jnp.float32,
    )
    teachers = [teacher_ref[pl.ds(pick, queries, stride=picks), :] for pick in range(picks)]
    students = [student[pl.ds(pick, queries, stride=picks), :] for pick in range(picks)]
    raised = sum(jnp.exp(scores) for scores in teachers)
    log_total = jnp.log(jnp.sum(raised, axis=1, keepdims=True))
    terms = 0.0
    for scores, guesses in zip(teachers, students):
        logp = scores - log_total
        terms = terms + jnp.exp(logp) * (logp - guesses)
    raised = sum(jnp.exp(guesses) for guesses in students)
    loss = jnp.sum(terms, axis=1, keepdims=True) + jnp.log(
        jnp.sum(raised, axis=1, keepdims=True)
    )
    out_ref[...] = jnp.broadcast_to(loss, (queries, 128)).T[:1]


def scored_loss(query_hidden, query_proj, passages, teacher, neg_blocks):
    dp = lax.axis_size("dp")
    mp = lax.axis_size("mp")
    queries, tokens, features = query_hidden.shape
    embed = query_proj.shape[1]
    picks = neg_blocks.shape[1]
    rows = queries * picks
    capacity = 2
    share = tokens // mp
    own_count, passage_tokens, _ = passages.shape
    count = own_count * mp

    partial = pl.pallas_call(
        project_kernel,
        out_shape=jax.ShapeDtypeStruct((mp, queries, share, embed), jnp.bfloat16),
        in_specs=[VMEM, VMEM],
        out_specs=VMEM,
        name="project",
    )(query_hidden.reshape(queries * tokens, features), query_proj)
    partial = lax.all_to_all(
        partial.reshape(mp, queries * share, embed), "mp", 0, 0, tiled=True
    ).reshape(mp, queries, share, embed)

    own_vecs = pl.pallas_call(
        passage_kernel,
        out_shape=out_vmem((own_count * passage_tokens, embed), jnp.bfloat16),
        in_specs=[VMEM],
        out_specs=VMEM,
        compiler_params=LIMIT,
        name="passages",
    )(passages.reshape(own_count * passage_tokens, embed))
    up = [(place, (place + 1) % mp) for place in range(mp)]
    down = [(place, (place + mp - 1) % mp) for place in range(mp)]
    below = lax.ppermute(own_vecs, "mp", up)
    above = lax.ppermute(own_vecs, "mp", down)
    opposite = lax.ppermute(below, "mp", up)

    owners = neg_blocks.reshape(rows)
    row_ids = jnp.arange(rows, dtype=jnp.int32)
    earlier = (owners[:, None] == owners[None, :]) & (row_ids[None, :] < row_ids[:, None])
    ranks = jnp.sum(earlier.astype(jnp.int32), axis=1)
    slot_ids = owners * capacity + ranks
    outgoing = pl.pallas_call(
        pack_kernel,
        out_shape=out_vmem((dp, capacity * share, embed), jnp.bfloat16),
        in_specs=[SMEM, VMEM],
        out_specs=VMEM,
        scratch_shapes=[
            pltpu.VMEM((queries, share, embed), jnp.float32),
            pltpu.VMEM((dp * capacity, share, embed), jnp.float32),
        ],
        compiler_params=LIMIT,
        name="pack",
    )(slot_ids, in_vmem(partial))
    arrived = lax.all_to_all(outgoing, "dp", 0, 0, tiled=True)

    turned, near = pl.pallas_call(
        functools.partial(near_kernel, capacity),
        out_shape=[
            out_vmem((share, capacity * dp, embed), jnp.bfloat16),
            out_vmem((count // 2, capacity * dp), jnp.float32),
        ],
        in_specs=[VMEM] * 3,
        out_specs=[VMEM] * 2,
        scratch_shapes=[
            pltpu.VMEM((dp * capacity * share, embed), jnp.float32),
            pltpu.VMEM((share, count // 2, 8, dp * capacity), jnp.float32),
        ],
        compiler_params=LIMIT,
        name="score_near",
    )(in_vmem(arrived.reshape(dp * capacity * share, embed)), in_vmem(own_vecs), in_vmem(below))
    scores = pl.pallas_call(
        functools.partial(far_kernel, capacity),
        out_shape=jax.ShapeDtypeStruct((dp * mp, capacity * count), jnp.float32),
        in_specs=[VMEM] * 4,
        out_specs=VMEM,
        scratch_shapes=[
            pltpu.VMEM((count, capacity * dp), jnp.float32),
            pltpu.VMEM((share, count // 2, 8, dp * capacity), jnp.float32),
        ],
        compiler_params=LIMIT,
        name="score_far",
    )(in_vmem(turned), in_vmem(opposite), in_vmem(above), in_vmem(near))
    scores, slot_row, teacher_rows = lax.optimization_barrier(
        (scores, slot_ids.reshape(1, rows), teacher.reshape(rows, count))
    )
    returned = lax.all_to_all(
        scores.reshape(dp * mp, 1, capacity * count), ("dp", "mp"), 0, 0, tiled=True
    ).reshape(dp * mp, capacity * count)

    loss = pl.pallas_call(
        loss_kernel,
        out_shape=jax.ShapeDtypeStruct((1, queries), jnp.float32),
        in_specs=[VMEM] * 3,
        out_specs=VMEM,
        scratch_shapes=[pltpu.VMEM((rows, count), jnp.float32)],
        compiler_params=LIMIT,
        name="loss",
    )(slot_row, in_vmem(returned), teacher_rows)
    return loss.reshape(queries)


def solution(mesh):
    in_specs = (
        P("dp", None, "mp"),
        P("mp", None),
        P(("dp", "mp"), None, None),
        P("dp", None, None),
        P("dp", None),
    )
    return jax.shard_map(
        scored_loss, mesh=mesh, in_specs=in_specs, out_specs=P("dp"), check_vma=False
    )
```
